256 devices in a mesh: lat: 8 (over z), lon: 32 (over y, x, core).
Axes of the slice: x: 4, y: 4, z: 8, core: 2. Of those that a mesh axis runs over, the one named last changes fastest.
Arguments:
- u_wind: float32 [1440, 32, 128], P('lon', 'lat'), may hold values from -6 to 6
- v_wind: float32 [1440, 32, 128], P('lon', 'lat'), may hold values from -6 to 6
- height: float32 [1440, 32, 128], P('lon', 'lat'), may hold values from -6 to 6
- wave_speed: float32 [128], replicated, may hold values from 0.1 to 0.4
- cutoff: int32 [32], replicated, may hold values from 1 to 720, as said below
Outputs:
- u_next: float32 [1440, 32, 128], P('lon', 'lat')
- v_next: float32 [1440, 32, 128], P('lon', 'lat')
- h_next: float32 [1440, 32, 128], P('lon', 'lat')
The draws below stay inside these ranges and needn't reach their ends.
Inputs may be any that keep to these rules, and one draw needn't show every extreme that they name: `cutoff`: rows 8 to 23, within 45 degrees of the equator, hold 720, which keeps every wavenumber; the other rows hold smaller values, 1 on the two outermost rows.
All inputs are finite; a program needn't handle non-finite values.
Results may differ from the reference program's by a relative error of at most 0.00005.
Values sent between devices are 32-bit elements; how exact they have to be, the bound alone decides.
No kernel may reach another device: no remote copies, remote signals or barrier semaphores. Data moves between devices by JAX's collectives and lax.ppermute only.
A program may use at most 64 MiB of HBM per device.

```python
import math
import jax
import jax.numpy as jnp

NLON = 1440
LEV = 128
NLAT = 32


def draw_cutoff(key, part):
    row_ids = jnp.arange(NLAT, dtype=jnp.int32)
    pole_dist = jnp.minimum(row_ids, NLAT - 1 - row_ids)
    quarter = NLAT // 4
    half_modes = NLON // 2
    base_cut = 1 + pole_dist * (half_modes - 1) // quarter
    jitter = jax.random.randint(key, (NLAT,), 0, 1 + half_modes // 16, dtype=jnp.int32)
    jitter = jitter * (pole_dist > 0).astype(jnp.int32)
    polar_cut = jnp.minimum(base_cut + jitter, half_modes)
    return jnp.where(pole_dist >= quarter, half_modes, polar_cut).astype(jnp.int32)


def level_of(own_key, extent, shards, smallest, top_value):
    level, own = 1.0, jax.random.fold_in(own_key, 6)
    for position, blocks in shards:
        steps = jnp.exp(jax.random.uniform(jax.random.fold_in(own, position), (blocks,), jnp.float32, smallest / len(shards), top_value / len(shards)))
        level = level * jnp.repeat(steps, extent[position] // blocks).reshape([-1 if axis == position else 1 for axis in range(len(extent))])
    return level


def bell_draw(key, extent, deviation, limit, shards=(), held_as=jnp.bfloat16):
    loudness = level_of(key, extent, shards, -0.22, 0.18) if shards else 1.0
    entries = jax.random.normal(key, extent, jnp.float32) * deviation * loudness
    return jnp.minimum(jnp.maximum(entries, -limit), limit).astype(held_as)


def setup_inputs(seed: int = 0) -> dict:
    seeds = jax.random.split(jax.random.key(seed), 6)
    return {
        "u_wind": bell_draw(seeds[0], (NLON, NLAT, LEV), 1.0, 6.0, ((0, 32), (1, 8)), jnp.float32),
        "v_wind": bell_draw(seeds[1], (NLON, NLAT, LEV), 1.0, 6.0, ((0, 32), (1, 8)), jnp.float32),
        "height": bell_draw(seeds[2], (NLON, NLAT, LEV), 1.0, 6.0, ((0, 32), (1, 8)), jnp.float32),
        "wave_speed": jnp.clip(jnp.exp(jax.random.uniform(seeds[3], (LEV,), jnp.float32, math.log(0.1), math.log(0.4))), 0.1, 0.4),
        "cutoff": draw_cutoff(jax.random.fold_in(seeds[5], 71), 0),
    }


coriolis_rate = 0.25


def reference(u_wind, v_wind, height, wave_speed, cutoff):
    row_ids = jnp.arange(NLAT, dtype=jnp.int32)
    latitude = 0.5 * math.pi - (row_ids.astype(jnp.float32) + 0.5) * (math.pi / NLAT)
    cos_lat = jnp.cos(latitude)[:, None]
    sin_lat = jnp.sin(latitude)[:, None]
    stretch = (NLON / (2.0 * NLAT)) / cos_lat
    speed_col = wave_speed[None, None, :]
    wavenum = jnp.arange(NLON // 2 + 1, dtype=jnp.int32)
    keep_mask = (wavenum[:, None] <= cutoff[None, :])[:, :, None]

    def smooth(field):
        spectrum = jnp.fft.rfft(field, axis=0)
        spectrum = jnp.where(keep_mask, spectrum, 0.0)
        return jnp.fft.irfft(spectrum, n=NLON, axis=0).astype(jnp.float32)

    def zonal(field):
        return (jnp.roll(field, -1, 0) - jnp.roll(field, 1, 0)) * 0.5

    def merid(field):
        padded = jnp.pad(field, ((0, 0), (1, 1), (0, 0)))
        return (padded[:, :-2, :] - padded[:, 2:, :]) * 0.5

    def tendency(u_now, v_now, h_now):
        zonal_u = zonal(u_now)
        zonal_h = zonal(h_now)
        merid_vc = merid(v_now * cos_lat)
        merid_h = merid(h_now)
        tend_u = coriolis_rate * sin_lat * v_now - speed_col * (stretch * zonal_h)
        tend_v = -coriolis_rate * sin_lat * u_now - speed_col * merid_h
        tend_h = -speed_col * (stretch * zonal_u + merid_vc / cos_lat)
        return (smooth(tend_u), smooth(tend_v), smooth(tend_h))

    fields = (u_wind, v_wind, height)
    change = tendency(u_wind, v_wind, height)
    first = [fields[n] + change[n] for n in range(3)]
    change = tendency(first[0], first[1], first[2])
    second = [0.75 * fields[n] + 0.25 * (first[n] + change[n]) for n in range(3)]
    change = tendency(second[0], second[1], second[2])
    third = [(1.0 / 3.0) * fields[n] + (2.0 / 3.0) * (second[n] + change[n]) for n in range(3)]
    return (third[0], third[1], third[2])
```

```python
import functools
import math

import jax
import jax.numpy as jnp
import numpy as np
from jax import lax
from jax.experimental import pallas as pl
from jax.experimental.pallas import tpu as pltpu
from jax.sharding import Mesh
from jax.sharding import PartitionSpec as P

LON = ("lon_0", "lon_1", "lon_2")

NB = 32
NR = 45
PTS = NB * NR
NK = NB // 2 + 1
ST = 48
ROWS = 4
HALO = 3
LV = 4
OWN = ROWS * ST
WIDE = 512
UP0 = WIDE - HALO * ST
DN1 = OWN + HALO * ST
PACK = 8 * ST
HI = lax.Precision.HIGHEST


def host_tables(bands):
    r = np.arange(NR)
    ang = 2.0 * np.pi * np.outer(r, r) / NR
    fwd_c = np.zeros((OWN, 256))
    fwd_s = np.zeros((OWN, 256))
    inv_c = np.zeros((256, OWN))
    inv_s = np.zeros((256, OWN))
    for j in range(ROWS):
        at = slice(j * ST, j * ST + NR)
        fwd_c[at, at] = np.cos(ang)
        fwd_s[at, at] = np.sin(ang)
        inv_c[at, at] = np.cos(ang) / PTS
        inv_s[at, at] = np.sin(ang) / PTS
    twid = np.zeros((NK, 2, OWN))
    for k in range(NK):
        for j in range(ROWS):
            at = slice(j * ST, j * ST + NR)
            twid[k, 0, at] = np.cos(2.0 * np.pi * k * r / PTS)
            twid[k, 1, at] = np.sin(2.0 * np.pi * k * r / PTS)
    row_of = np.full(WIDE, -100)
    k2_of = np.zeros(WIDE, np.int64)
    for row in range(-HALO, ROWS + HALO):
        first = row * ST if row >= 0 else WIDE + row * ST
        row_of[first : first + NR] = row
        k2_of[first : first + NR] = r
    wav = np.arange(NK)[:, None] + NB * k2_of[None, :]
    slope = np.sin(2.0 * np.pi * wav / PTS)
    least = np.minimum(wav, PTS - wav)
    total = bands * ROWS
    per_band = np.zeros((bands, 4, WIDE))
    for z in range(bands):
        g = z * ROWS + row_of
        ok = (g >= 0) & (g < total) & (row_of > -100)
        half_pi = np.float32(0.5 * math.pi)
        lat = half_pi - (g.astype(np.float32) + np.float32(0.5)) * np.float32(math.pi / total)
        cos = np.cos(lat, dtype=np.float32)
        sin = np.sin(lat, dtype=np.float32)
        cos = np.where(ok, cos, 1.0)
        per_band[z, 0] = np.where(ok, 0.25 * sin, 0.0)
        per_band[z, 1] = np.where(ok, PTS / (2.0 * total) / cos, 0.0)
        per_band[z, 2] = np.where(ok, cos, 0.0)
        per_band[z, 3] = np.where(ok, 0.5 / cos, 0.0)
    f32 = lambda a: jnp.asarray(np.asarray(a, np.float32))
    return (
        tuple(f32(a) for a in (fwd_c, fwd_s, inv_c, inv_s, twid, slope[:, None, :], per_band)),
        jnp.asarray(least[:, None, :].astype(np.int32)),
    )


def real_fft(xs):
    n = len(xs)
    if n == 1:
        return [(xs[0], None)]
    even, odd = real_fft(xs[0::2]), real_fft(xs[1::2])
    out = [None] * (n // 2 + 1)
    for k in range(n // 4 + 1 if n > 2 else 1):
        er, ei = even[k]
        orr, oi = odd[k]
        if k == 0:
            out[0] = (er + orr, None)
            out[n // 2] = (er - orr, None)
        elif 4 * k == n:
            out[k] = (er, -orr)
        else:
            c, s = math.cos(2 * math.pi * k / n), math.sin(2 * math.pi * k / n)
            if oi is None:
                tr, ti = orr * c, orr * (-s)
            elif 8 * k == n:
                tr, ti = (orr + oi) * c, (oi - orr) * c
            else:
                tr, ti = orr * c + oi * s, oi * c - orr * s
            if ei is None:
                out[k] = (er + tr, ti)
                out[n // 2 - k] = (er - tr, ti)
            else:
                out[k] = (er + tr, ei + ti)
                out[n // 2 - k] = (er - tr, ti - ei)
    return out


def real_ifft(spec):
    n = 2 * (len(spec) - 1)
    if n == 2:
        return [spec[0][0] + spec[1][0], spec[0][0] - spec[1][0]]
    even, odd = [None] * (n // 4 + 1), [None] * (n // 4 + 1)
    for k in range(n // 4 + 1):
        ar, ai = spec[k]
        if k == 0:
            br = spec[n // 2][0]
            even[0] = (ar + br, None)
            odd[0] = (ar - br, None)
        elif 4 * k == n:
            even[k] = (2.0 * ar, None)
            odd[k] = (-2.0 * ai, None)
        else:
            br, bi = spec[n // 2 - k]
            even[k] = (ar + br, ai - bi)
            dr, di = ar - br, ai + bi
            c, s = math.cos(2 * math.pi * k / n), math.sin(2 * math.pi * k / n)
            if 8 * k == n:
                odd[k] = ((dr - di) * c, (dr + di) * c)
            else:
                odd[k] = (dr * c - di * s, dr * s + di * c)
    xe, xo = real_ifft(even), real_ifft(odd)
    out = []
    for a, b in zip(xe, xo):
        out += [a, b]
    return out


def pack_kernel(u_ref, v_ref, h_ref, o_ref, tmp):
    tmp[...] = jnp.zeros_like(tmp)
    for f, ref in enumerate((u_ref, v_ref, h_ref)):
        for j in range(ROWS):
            tmp[f, j * ST : j * ST + NR, :] = ref[:, j, :]
    for f in range(3):
        turned = tmp[f].T
        for l in range(LV):
            o_ref[:, f, l, :] = turned[l * NB : (l + 1) * NB, :OWN]


def forward_kernel(z_ref, c_ref, s_ref, tw_ref, own_ref, up_ref, dn_ref, x_ref, xi_ref):
    for f in range(3):
        spec = real_fft([z_ref[d, f] for d in range(NB)])
        for k in range(NK):
            a, b = spec[k]
            c, s = tw_ref[k, 0:1, :], tw_ref[k, 1:2, :]
            if b is None:
                re, im = a * c, -(a * s)
            else:
                re, im = a * c + b * s, b * c - a * s
            x_ref[f, k * 8 : k * 8 + 4, :] = re
            x_ref[f, k * 8 + 4 : k * 8 + 8, :] = im
            xi_ref[f, k * 8 : k * 8 + 4, :] = im
            xi_ref[f, k * 8 + 4 : k * 8 + 8, :] = -re
    got = []
    for f in range(3):
        y = jnp.dot(x_ref[f], c_ref[...], precision=HI, preferred_element_type=jnp.float32)
        y = y + jnp.dot(xi_ref[f], s_ref[...], precision=HI, preferred_element_type=jnp.float32)
        own_ref[f] = y
    for k in range(NK):
        at = slice(k * 8, k * 8 + 8)
        pad = jnp.zeros((8, 128), jnp.float32)
        u, v, h = (jnp.concatenate([own_ref[f, at, :], pad], axis=1) for f in range(3))
        lane = lax.broadcasted_iota(jnp.int32, (8, PACK), 1)
        roll = lambda a, n: pltpu.roll(a, n % PACK, 1)
        up_ref[at, :] = jnp.where(
            lane < 2 * ST, roll(u, -2 * ST), jnp.where(lane < 5 * ST, roll(v, ST), roll(h, 4 * ST))
        )
        dn_ref[at, :] = jnp.where(
            lane < 2 * ST, u, jnp.where(lane < 5 * ST, roll(v, 2 * ST), roll(h, 5 * ST))
        )


def step_kernel(
    cut_ref, speed_ref, own_ref, up_ref, dn_ref, slope_ref, least_ref, band_ref,
    c_ref, s_ref, tw_ref, w_ref, y_ref, pc_ref, ps_ref,
):
    z = lax.axis_index("lat")
    p = (lax.axis_index("lon_0") * 4 + lax.axis_index("lon_1")) * 2 + lax.axis_index("lon_2")
    total = cut_ref.shape[0]
    lane1 = lax.broadcasted_iota(jnp.int32, (1, WIDE), 1)
    cut = jnp.full((1, WIDE), -1, jnp.int32)
    for row in range(-HALO, ROWS + HALO):
        g = z * ROWS + row
        inside = jnp.logical_and(g >= 0, g < total)
        value = jnp.where(inside, cut_ref[jnp.clip(g, 0, total - 1)], -1)
        first = row * ST if row >= 0 else WIDE + row * ST
        cut = jnp.where(jnp.logical_and(lane1 >= first, lane1 < first + NR), value, cut)
    sub = lax.broadcasted_iota(jnp.int32, (8, WIDE), 0)
    lane = lax.broadcasted_iota(jnp.int32, (8, WIDE), 1)
    speed = jnp.zeros((8, WIDE), jnp.float32)
    for l in range(LV):
        speed = jnp.where(sub % LV == l, speed_ref[l * NB + p], speed)
    turn_speed = jnp.where(sub < LV, -speed, speed)
    cor = band_ref[z, 0:1, :]
    stretch = band_ref[z, 1:2, :]
    cosl = band_ref[z, 2:3, :]
    half_sec = band_ref[z, 3:4, :]
    roll = lambda a, n: pltpu.roll(a, n % WIDE, 1)

    def body(k, carry):
        at = pl.ds(pl.multiple_of(k * 8, 8), 8)
        up = jnp.concatenate([up_ref[at, :], jnp.zeros((8, 128), jnp.float32)], axis=1)
        dn = jnp.concatenate([dn_ref[at, :], jnp.zeros((8, 128), jnp.float32)], axis=1)
        fields = []
        for f, (up_by, dn_by, n) in enumerate(
            ((-2 * ST, 4 * ST, 2), (-5 * ST, 2 * ST, 3), (-8 * ST, -ST, 3))
        ):
            own = jnp.concatenate([own_ref[f, at, :], jnp.zeros((8, 256), jnp.float32)], axis=1)
            q = jnp.where(lane >= WIDE - n * ST, roll(up, up_by), own)
            q = jnp.where(jnp.logical_and(lane >= OWN, lane < OWN + n * ST), roll(dn, dn_by), q)
            fields.append(q)
        keep = least_ref[k] <= cut
        zs = slope_ref[k] * stretch

        def apply(u, v, h):
            su = pltpu.roll(u, LV, 0)
            sh = pltpu.roll(h, LV, 0)
            vc = v * cosl
            dh = (roll(h, ST) - roll(h, -ST)) * 0.5
            dv = (roll(vc, ST) - roll(vc, -ST)) * half_sec
            tu = cor * v - turn_speed * (zs * sh)
            tv = -(cor * u) - speed * dh
            th = -(turn_speed * (zs * su)) - speed * dv
            return tuple(jnp.where(keep, t, 0.0) for t in (tu, tv, th))

        change = apply(*fields)
        first = [q + t for q, t in zip(fields, change)]
        change = apply(*first)
        second = [0.75 * q + 0.25 * (a + t) for q, a, t in zip(fields, first, change)]
        change = apply(*second)
        for f in range(3):
            gain = jnp.where(keep, second[f] - fields[f], 0.0) + change[f]
            y_ref[f, at, :] = (2.0 / 3.0) * gain[:, :256]
        return carry

    lax.fori_loop(0, NK, body, 0)
    for f in range(3):
        pc_ref[f] = jnp.dot(y_ref[f], c_ref[...], precision=HI, preferred_element_type=jnp.float32)
        ps_ref[f] = jnp.dot(y_ref[f], s_ref[...], precision=HI, preferred_element_type=jnp.float32)
    for f in range(3):
        spec = []
        for k in range(NK):
            re, im = slice(k * 8, k * 8 + 4), slice(k * 8 + 4, k * 8 + 8)
            a = pc_ref[f, re, :] - ps_ref[f, im, :]
            b = pc_ref[f, im, :] + ps_ref[f, re, :]
            c, s = tw_ref[k, 0:1, :], tw_ref[k, 1:2, :]
            spec.append((a * c - b * s, a * s + b * c))
        for d, value in enumerate(real_ifft(spec)):
            w_ref[d, f] = value


def unpack_kernel(w_ref, u_ref, v_ref, h_ref, uo_ref, vo_ref, ho_ref):
    for f, (ref, out) in enumerate(((u_ref, uo_ref), (v_ref, vo_ref), (h_ref, ho_ref))):
        block = jnp.concatenate([w_ref[:, f, l, :] for l in range(LV)], axis=0)
        turned = block.T
        for j in range(ROWS):
            out[:, j, :] = ref[:, j, :] + turned[j * ST : j * ST + NR, :]


def vmem(count):
    return [pl.BlockSpec(memory_space=pltpu.VMEM)] * count


def smem(count):
    return [pl.BlockSpec(memory_space=pltpu.SMEM)] * count


def shaped(*dims):
    return jax.ShapeDtypeStruct(dims, jnp.float32)


def shards(u_wind, v_wind, height, wave_speed, cutoff):
    bands = lax.axis_size("lat")
    (fwd_c, fwd_s, inv_c, inv_s, twid, slope, per_band), least = host_tables(bands)
    packed = pl.pallas_call(
        pack_kernel,
        out_shape=shaped(NB, 3, LV, OWN),
        in_specs=vmem(3),
        out_specs=vmem(1)[0],
        scratch_shapes=[pltpu.VMEM((3, 256, 128), jnp.float32)],
        name="pack",
    )(u_wind, v_wind, height)
    circles = lax.all_to_all(packed, LON, 0, 0, tiled=True)
    own, up, dn = pl.pallas_call(
        forward_kernel,
        out_shape=(shaped(3, NK * 8, 256), shaped(NK * 8, PACK), shaped(NK * 8, PACK)),
        in_specs=vmem(4),
        out_specs=tuple(vmem(3)),
        scratch_shapes=[pltpu.VMEM((3, NK * 8, OWN), jnp.float32)] * 2,
        name="forward",
    )(circles, fwd_c, fwd_s, twid)
    south = [(i, i + 1) for i in range(bands - 1)]
    north = [(b, a) for a, b in south]
    up = lax.ppermute(up, "lat", south)
    dn = lax.ppermute(dn, "lat", north)
    waves = pl.pallas_call(
        step_kernel,
        out_shape=shaped(NB, 3, LV, OWN),
        in_specs=smem(2) + vmem(9),
        out_specs=vmem(1)[0],
        scratch_shapes=[pltpu.VMEM((3, NK * 8, 256), jnp.float32)]
        + [pltpu.VMEM((3, NK * 8, OWN), jnp.float32)] * 2,
        name="sections",
    )(cutoff, wave_speed, own, up, dn, slope, least, per_band, inv_c, inv_s, twid)
    waves = lax.all_to_all(waves, LON, 0, 0, tiled=True)
    return pl.pallas_call(
        unpack_kernel,
        out_shape=tuple(shaped(NR, ROWS, u_wind.shape[2]) for _ in range(3)),
        in_specs=vmem(4),
        out_specs=tuple(vmem(3)),
        name="unpack",
    )(waves, u_wind, v_wind, height)


def solution(mesh):
    split = Mesh(
        mesh.devices.reshape(mesh.shape["lat"], 4, 4, 2), ("lat", "lon_0", "lon_1", "lon_2")
    )
    return jax.shard_map(
        shards,
        mesh=split,
        in_specs=(P(LON, "lat", None), P(LON, "lat", None), P(LON, "lat", None), P(), P()),
        out_specs=(P(LON, "lat", None), P(LON, "lat", None), P(LON, "lat", None)),
        check_vma=False,
    )
```

```python
import math

import jax
import jax.numpy as jnp
import ml_dtypes
import numpy as np
from jax import lax
from jax.experimental import pallas as pl
from jax.experimental.pallas import tpu as pltpu
from jax.sharding import Mesh
from jax.sharding import PartitionSpec as P

LON = ("lon_0", "lon_1", "lon_2")

NB = 32
NR = 45
PTS = NB * NR
NK = NB // 2 + 1
PAIRS = (NK + 1) // 2
ROWS = 4
HALO = 3
LV = 4
FAR = 1 << 20
PARAMS = pltpu.CompilerParams(vmem_limit_bytes=12 << 20)


def split_three(a):
    high = a.astype(ml_dtypes.bfloat16)
    rest = a - high.astype(np.float64)
    mid = rest.astype(ml_dtypes.bfloat16)
    low = (rest - mid.astype(np.float64)).astype(ml_dtypes.bfloat16)
    return high, mid, low


def host_tables(bands):
    r = np.arange(NR)
    ang = 2.0 * np.pi * np.outer(r, r) / NR
    dft = np.zeros((128, 256))
    twid = np.zeros((NK, 2, 128))
    for side in range(2):
        at = slice(side * 64, side * 64 + NR)
        dft[at, at] = np.cos(ang)
        dft[at, 128 + side * 64 : 128 + side * 64 + NR] = np.sin(ang)
        for k in range(NK):
            twid[k, 0, at] = np.cos(2.0 * np.pi * k * r / PTS)
            twid[k, 1, at] = np.sin(2.0 * np.pi * k * r / PTS)
    high, mid, low = split_three(dft)
    dft = np.concatenate([high, high, mid, mid, low, high], axis=0)
    lane = np.arange(128)
    k1 = 2 * np.arange(PAIRS)[:, None] + lane[None, :] // 64
    wav = k1 + NB * (lane % 64)[None, :]
    ok = (k1 < NK) & (lane % 64 < NR)[None, :]
    slope = np.where(ok, np.sin(2.0 * np.pi * wav / PTS), 0.0)
    least = np.where(ok, np.minimum(wav, PTS - wav), FAR)
    total = bands * ROWS
    per_band = np.zeros((bands, 4, 16, 128), np.float32)
    row = np.arange(-HALO, ROWS + HALO)
    half_pi = np.float32(0.5 * math.pi)
    for z in range(bands):
        g = z * ROWS + row
        ok = (g >= 0) & (g < total)
        lat = half_pi - (g.astype(np.float32) + np.float32(0.5)) * np.float32(math.pi / total)
        cos = np.where(ok, np.cos(lat, dtype=np.float32), np.float32(1.0))
        sin = np.sin(lat, dtype=np.float32)
        rows = (0.25 * sin, PTS / (2.0 * total) / cos, cos, 0.5 / cos)
        for c, value in enumerate(rows):
            per_band[z, c, : len(row), :] = np.where(ok, value, 0.0)[:, None]
    f32 = lambda a: jnp.asarray(np.asarray(a, np.float32))
    return (
        jnp.asarray(dft),
        f32(twid),
        f32(twid / PTS),
        f32(slope[:, None, :]),
        jnp.asarray(least[:, None, :].astype(np.int32)),
        f32(per_band),
    )


def real_fft(xs):
    n = len(xs)
    if n == 1:
        return [(xs[0], None)]
    even, odd = real_fft(xs[0::2]), real_fft(xs[1::2])
    out = [None] * (n // 2 + 1)
    for k in range(n // 4 + 1 if n > 2 else 1):
        er, ei = even[k]
        orr, oi = odd[k]
        if k == 0:
            out[0] = (er + orr, None)
            out[n // 2] = (er - orr, None)
        elif 4 * k == n:
            out[k] = (er, -orr)
        else:
            c, s = math.cos(2 * math.pi * k / n), math.sin(2 * math.pi * k / n)
            if oi is None:
                tr, ti = orr * c, orr * (-s)
            elif 8 * k == n:
                tr, ti = (orr + oi) * c, (oi - orr) * c
            else:
                tr, ti = orr * c + oi * s, oi * c - orr * s
            if ei is None:
                out[k] = (er + tr, ti)
                out[n // 2 - k] = (er - tr, ti)
            else:
                out[k] = (er + tr, ei + ti)
                out[n // 2 - k] = (er - tr, ti - ei)
    return out


def real_ifft(spec):
    n = 2 * (len(spec) - 1)
    if n == 2:
        return [spec[0][0] + spec[1][0], spec[0][0] - spec[1][0]]
    even, odd = [None] * (n // 4 + 1), [None] * (n // 4 + 1)
    for k in range(n // 4 + 1):
        ar, ai = spec[k]
        if k == 0:
            br = spec[n // 2][0]
            even[0] = (ar + br, None)
            odd[0] = (ar - br, None)
        elif 4 * k == n:
            even[k] = (2.0 * ar, None)
            odd[k] = (-2.0 * ai, None)
        else:
            br, bi = spec[n // 2 - k]
            even[k] = (ar + br, ai - bi)
            dr, di = ar - br, ai + bi
            c, s = math.cos(2 * math.pi * k / n), math.sin(2 * math.pi * k / n)
            if 8 * k == n:
                odd[k] = ((dr - di) * c, (dr + di) * c)
            else:
                odd[k] = (dr * c - di * s, dr * s + di * c)
    xe, xo = real_ifft(even), real_ifft(odd)
    out = []
    for a, b in zip(xe, xo):
        out += [a, b]
    return out


def pack_kernel(u_hbm, v_hbm, h_hbm, cut_hbm, speed_hbm, o_ref, cut_ref, speed_ref, raw, tmp, cut, speed, sem):
    copies = [
        pltpu.make_async_copy(src, raw.at[f], sem.at[f])
        for f, src in enumerate((u_hbm, v_hbm, h_hbm))
    ]
    copies.append(pltpu.make_async_copy(cut_hbm, cut, sem.at[3]))
    copies.append(pltpu.make_async_copy(speed_hbm, speed, sem.at[4]))
    for copy in copies:
        copy.start()
    tmp[...] = jnp.zeros_like(tmp)
    for f in range(3):
        copies[f].wait()
        for j in range(ROWS):
            tmp[f, j // 2, j % 2 * 64 : j % 2 * 64 + NR, :] = raw[f, :, j, :]
        for half in range(2):
            turned = tmp[f, half].T
            for l in range(LV):
                o_ref[:, half * LV + l, f * 128 : (f + 1) * 128] = turned[l * NB : (l + 1) * NB, :]
    copies[3].wait()
    copies[4].wait()
    z = lax.axis_index("lat")
    p = (lax.axis_index("lon_0") * 4 + lax.axis_index("lon_1")) * 2 + lax.axis_index("lon_2")
    total = cut.shape[0]
    sub = lax.broadcasted_iota(jnp.int32, (16, 128), 0)
    rows = jnp.full((16, 128), -1, jnp.int32)
    for i in range(ROWS + 2 * HALO):
        g = z * ROWS + i - HALO
        inside = jnp.logical_and(g >= 0, g < total)
        rows = jnp.where(sub == i, jnp.where(inside, cut[jnp.clip(g, 0, total - 1)], -1), rows)
    cut_ref[...] = rows
    sub = lax.broadcasted_iota(jnp.int32, (8, 128), 0)
    value = jnp.zeros((8, 128), jnp.float32)
    for l in range(LV):
        value = jnp.where(sub % LV == l, speed[l * NB + p], value)
    speed_ref[...] = value


def split_store(ref, at, re, im):
    x = jnp.concatenate([re, im], axis=0)
    high = x.astype(jnp.bfloat16)
    rest = x - high.astype(jnp.float32)
    mid = rest.astype(jnp.bfloat16)
    low = (rest - mid.astype(jnp.float32)).astype(jnp.bfloat16)
    for i, part in enumerate((high, mid, high, mid, high, low)):
        ref[at, i * 128 : (i + 1) * 128] = part


def swap_sub(a, b, low):
    return jnp.where(low, a, pltpu.roll(b, 4, 0)), jnp.where(low, pltpu.roll(a, 4, 0), b)


def swap_lane(a, b, low):
    return jnp.where(low, a, pltpu.roll(b, 64, 1)), jnp.where(low, pltpu.roll(a, 64, 1), b)


def halves():
    sub = lax.broadcasted_iota(jnp.int32, (8, 128), 0) < 4
    lane = lax.broadcasted_iota(jnp.int32, (8, 128), 1)
    return sub, lane < 64, lane % 64


def forward_kernel(z_ref, dft_ref, tw_ref, own_ref, up_ref, dn_ref, x_ref, y_ref):
    for f in range(3):
        spec = real_fft([z_ref[d, :, f * 128 : (f + 1) * 128] for d in range(NB)])
        for k in range(NK):
            a, b = spec[k]
            c, s = tw_ref[k, 0:1, :], tw_ref[k, 1:2, :]
            if b is None:
                re, im = a * c, -(a * s)
            else:
                re, im = a * c + b * s, b * c - a * s
            split_store(x_ref, slice((f * NK + k) * 16, (f * NK + k) * 16 + 16), re, im)
    y_ref[...] = jnp.dot(x_ref[...], dft_ref[...], preferred_element_type=jnp.float32)
    sub, lane, inner = halves()
    for i in range(PAIRS):
        tiles = []
        for f in range(3):
            parts = []
            for k in (2 * i, 2 * i + 1):
                if k == NK:
                    parts.append((jnp.zeros((8, 128), jnp.float32),) * 2)
                    continue
                at = (f * NK + k) * 16
                re = y_ref[at : at + 8, :128] + y_ref[at + 8 : at + 16, 128:]
                im = y_ref[at + 8 : at + 16, :128] - y_ref[at : at + 8, 128:]
                parts.append(swap_sub(re, im, sub))
            rows = []
            for half in range(2):
                rows += swap_lane(parts[0][half], parts[1][half], lane)
            for j in range(ROWS):
                own_ref[(i * 3 + f) * ROWS + j] = rows[j]
            tiles.append(rows)
        u, v, h = tiles
        for ref, first in ((up_ref, 1), (dn_ref, 0)):
            main = v[first : first + 3] + h[first : first + 3]
            side = u[2:4] if first else u[0:2]
            for n in range(6):
                extra = pltpu.roll(side[n // 3], 48 - 16 * (n % 3), 1)
                ref[i * 6 + n] = jnp.where(inner < 48, main[n], extra)


def step_kernel(
    own_ref, up_ref, dn_ref, cut_ref, speed_ref, slope_ref, least_ref, band_ref, dft_ref, tw_ref,
    w_ref, x_ref, y_ref,
):
    z = lax.axis_index("lat")
    sub, lane, inner = halves()
    speed = speed_ref[...]
    turn_speed = jnp.where(sub, -speed, speed)
    half_speed = 0.5 * speed

    def body(i, carry):
        def received(ref):
            tiles = [ref[i * 6 + n] for n in range(6)]
            side = []
            for n in (0, 3):
                one, two, three = (pltpu.roll(tiles[n + c], 128 - 48 + 16 * c, 1) for c in range(3))
                side.append(jnp.where(inner < 16, one, jnp.where(inner < 32, two, three)))
            return side, tiles[:3], tiles[3:]

        above, below = received(up_ref), received(dn_ref)
        mine = [[own_ref[(i * 3 + f) * ROWS + j] for j in range(ROWS)] for f in range(3)]
        u = [None] + above[0] + mine[0] + below[0] + [None]
        v = above[1] + mine[1] + below[1]
        h = above[2] + mine[2] + below[2]
        start = (u, v, h)
        least = least_ref[i]
        wave = turn_speed * slope_ref[i]
        count = ROWS + 2 * HALO
        keep, zs = [None] * count, [None] * count
        for j in range(1, count - 1):
            keep[j] = jnp.where(least <= cut_ref[j : j + 1, :], 1.0, 0.0)
            zs[j] = wave * band_ref[z, 1, j : j + 1, :]

        def advance(state, margin, scale):
            su, sv, sh = state
            vc = [None] * count
            for j in range(margin - 1, count - margin + 1):
                vc[j] = sv[j] * band_ref[z, 2, j : j + 1, :]
            out = ([None] * count, [None] * count, [None] * count)
            for j in range(margin, count - margin):
                cor = band_ref[z, 0, j : j + 1, :]
                tu = cor * sv[j] - zs[j] * pltpu.roll(sh[j], 4, 0)
                tv = cor * su[j] + half_speed * (sh[j - 1] - sh[j + 1])
                th = zs[j] * pltpu.roll(su[j], 4, 0) + (speed * band_ref[z, 3, j : j + 1, :]) * (
                    vc[j - 1] - vc[j + 1]
                )
                if scale is None:
                    out[0][j], out[1][j], out[2][j] = keep[j] * tu, -keep[j] * tv, -keep[j] * th
                else:
                    m = keep[j] * scale
                    out[0][j] = u[j] + m * tu
                    out[1][j] = v[j] - m * tv
                    out[2][j] = h[j] - m * th
            return out

        gain = advance(advance(advance(start, 1, 1.0 / 3.0), 2, 0.5), 3, None)
        for f in range(3):
            rows = gain[f][HALO : HALO + ROWS]
            north, south = swap_lane(rows[0], rows[1], lane), swap_lane(rows[2], rows[3], lane)
            for side in range(2):
                re, im = swap_sub(north[side], south[side], sub)
                at = (f * 2 * PAIRS + side) * 16 + i * 32
                split_store(x_ref, pl.ds(at, 16), re, im)
        return carry

    for i in range(PAIRS):
        body(i, 0)
    y_ref[...] = jnp.dot(x_ref[...], dft_ref[...], preferred_element_type=jnp.float32)
    for f in range(3):
        spec = []
        for k in range(NK):
            at = (f * 2 * PAIRS + k) * 16
            a = y_ref[at : at + 8, :128] - y_ref[at + 8 : at + 16, 128:]
            b = y_ref[at + 8 : at + 16, :128] + y_ref[at : at + 8, 128:]
            c, s = tw_ref[k, 0:1, :], tw_ref[k, 1:2, :]
            spec.append((a * c - b * s, a * s + b * c))
        for d, value in enumerate(real_ifft(spec)):
            w_ref[d, :, f * 128 : (f + 1) * 128] = value


def unpack_kernel(w_ref, u_ref, v_ref, h_ref, u_hbm, v_hbm, h_hbm, out, sem):
    copies = []
    for f, (ref, hbm) in enumerate(((u_ref, u_hbm), (v_ref, v_hbm), (h_ref, h_hbm))):
        for half in range(2):
            block = [w_ref[:, half * LV + l, f * 128 : (f + 1) * 128] for l in range(LV)]
            turned = jnp.concatenate(block, axis=0).T
            for side in range(2):
                j = half * 2 + side
                out[f, :, j, :] = ref[:, j, :] + turned[side * 64 : side * 64 + NR, :]
        copies.append(pltpu.make_async_copy(out.at[f], hbm, sem.at[f]))
        copies[-1].start()
    for copy in copies:
        copy.wait()


def vmem(count):
    return [pl.BlockSpec(memory_space=pltpu.VMEM)] * count


def hbm(count):
    return [pl.BlockSpec(memory_space=pltpu.HBM)] * count


def shaped(*dims):
    return jax.ShapeDtypeStruct(dims, jnp.float32)


def shards(u_wind, v_wind, height, wave_speed, cutoff):
    bands = lax.axis_size("lat")
    dft, twid, twid_back, slope, least, per_band = host_tables(bands)
    levels = u_wind.shape[2]
    packed, cut_rows, speeds = pl.pallas_call(
        pack_kernel,
        out_shape=(
            shaped(NB, 2 * LV, 384),
            jax.ShapeDtypeStruct((16, 128), jnp.int32),
            shaped(8, 128),
        ),
        in_specs=hbm(5),
        out_specs=tuple(vmem(3)),
        scratch_shapes=[
            pltpu.VMEM((3, NR, ROWS, levels), jnp.float32),
            pltpu.VMEM((3, 2, 128, levels), jnp.float32),
            pltpu.SMEM(cutoff.shape, jnp.int32),
            pltpu.SMEM(wave_speed.shape, jnp.float32),
            pltpu.SemaphoreType.DMA((5,)),
        ],
        name="pack",
        compiler_params=PARAMS,
    )(*(pltpu.with_memory_space_constraint(a, pltpu.HBM) for a in (u_wind, v_wind, height, cutoff, wave_speed)))
    circles = lax.all_to_all(packed, LON, 0, 0, tiled=True)
    own, up, dn = pl.pallas_call(
        forward_kernel,
        out_shape=(
            shaped(PAIRS * 3 * ROWS, 8, 128),
            shaped(PAIRS * 6, 8, 128),
            shaped(PAIRS * 6, 8, 128),
        ),
        in_specs=vmem(3),
        out_specs=tuple(vmem(3)),
        scratch_shapes=[
            pltpu.VMEM((3 * NK * 16, 768), jnp.bfloat16),
            pltpu.VMEM((3 * NK * 16, 256), jnp.float32),
        ],
        name="forward",
        compiler_params=PARAMS,
    )(circles, dft, twid)
    south = [(i, i + 1) for i in range(bands - 1)]
    north = [(b, a) for a, b in south]
    up = lax.ppermute(up, "lat", south)
    dn = lax.ppermute(dn, "lat", north)
    waves = pl.pallas_call(
        step_kernel,
        out_shape=shaped(NB, 2 * LV, 384),
        in_specs=vmem(10),
        out_specs=vmem(1)[0],
        scratch_shapes=[
            pltpu.VMEM((3 * 2 * PAIRS * 16, 768), jnp.bfloat16),
            pltpu.VMEM((3 * 2 * PAIRS * 16, 256), jnp.float32),
        ],
        name="sections",
        compiler_params=PARAMS,
    )(own, up, dn, cut_rows, speeds, slope, least, per_band, dft, twid_back)
    waves = lax.all_to_all(waves, LON, 0, 0, tiled=True)
    return pl.pallas_call(
        unpack_kernel,
        out_shape=tuple(shaped(NR, ROWS, levels) for _ in range(3)),
        in_specs=vmem(4),
        out_specs=tuple(hbm(3)),
        scratch_shapes=[
            pltpu.VMEM((3, NR, ROWS, levels), jnp.float32),
            pltpu.SemaphoreType.DMA((3,)),
        ],
        name="unpack",
        compiler_params=PARAMS,
    )(waves, u_wind, v_wind, height)


def solution(mesh):
    split = Mesh(
        mesh.devices.reshape(mesh.shape["lat"], 4, 4, 2), ("lat", "lon_0", "lon_1", "lon_2")
    )
    return jax.shard_map(
        shards,
        mesh=split,
        in_specs=(P(LON, "lat", None), P(LON, "lat", None), P(LON, "lat", None), P(), P()),
        out_specs=(P(LON, "lat", None), P(LON, "lat", None), P(LON, "lat", None)),
        check_vma=False,
    )
```

```python
import math

import jax
import jax.numpy as jnp
import ml_dtypes
import numpy as np
from jax import lax
from jax.experimental import pallas as pl
from jax.experimental.pallas import tpu as pltpu
from jax.sharding import Mesh
from jax.sharding import PartitionSpec as P

LON = ("lon_0", "lon_1", "lon_2")

NB = 32
NR = 45
PTS = NB * NR
NK = NB // 2 + 1
PAIRS = (NK + 1) // 2
ROWS = 4
HALO = 3
LV = 4
SLOTS = 5
FAR = 1 << 20
PARAMS = pltpu.CompilerParams(vmem_limit_bytes=12 << 20)


def split_three(a):
    high = a.astype(ml_dtypes.bfloat16)
    rest = a - high.astype(np.float64)
    mid = rest.astype(ml_dtypes.bfloat16)
    low = (rest - mid.astype(np.float64)).astype(ml_dtypes.bfloat16)
    return high, mid, low


def host_tables(bands):
    r = np.arange(NR)
    ang = 2.0 * np.pi * np.outer(r, r) / NR
    dft = np.zeros((128, 256))
    twid = np.zeros((NK, 2, 128))
    for side in range(2):
        at = slice(side * 64, side * 64 + NR)
        dft[at, at] = np.cos(ang)
        dft[at, 128 + side * 64 : 128 + side * 64 + NR] = np.sin(ang)
        for k in range(NK):
            twid[k, 0, at] = np.cos(2.0 * np.pi * k * r / PTS)
            twid[k, 1, at] = np.sin(2.0 * np.pi * k * r / PTS)
    high, mid, low = split_three(dft)
    dft = np.concatenate([high, high, mid, mid, low, high], axis=0)
    lane = np.arange(128)
    k1 = 2 * np.arange(PAIRS)[:, None] + lane[None, :] // 64
    wav = k1 + NB * (lane % 64)[None, :]
    ok = (k1 < NK) & (lane % 64 < NR)[None, :]
    slope = np.where(ok, np.sin(2.0 * np.pi * wav / PTS), 0.0)
    least = np.where(ok, np.minimum(wav, PTS - wav), FAR)
    total = bands * ROWS
    per_band = np.zeros((bands, 4, 16, 128), np.float32)
    row = np.arange(-HALO, ROWS + HALO)
    half_pi = np.float32(0.5 * math.pi)
    for z in range(bands):
        g = z * ROWS + row
        ok = (g >= 0) & (g < total)
        lat = half_pi - (g.astype(np.float32) + np.float32(0.5)) * np.float32(math.pi / total)
        cos = np.where(ok, np.cos(lat, dtype=np.float32), np.float32(1.0))
        sin = np.sin(lat, dtype=np.float32)
        rows = (0.25 * sin, PTS / (2.0 * total) / cos, cos, 0.5 / cos)
        for c, value in enumerate(rows):
            per_band[z, c, : len(row), :] = np.where(ok, value, 0.0)[:, None]
    f32 = lambda a: jnp.asarray(np.asarray(a, np.float32))
    return (
        jnp.asarray(dft),
        f32(twid),
        f32(twid / PTS),
        f32(slope[:, None, :]),
        jnp.asarray(least[:, None, :].astype(np.int32)),
        f32(per_band),
    )


def real_fft(xs):
    n = len(xs)
    if n == 1:
        return [(xs[0], None)]
    even, odd = real_fft(xs[0::2]), real_fft(xs[1::2])
    out = [None] * (n // 2 + 1)
    for k in range(n // 4 + 1 if n > 2 else 1):
        er, ei = even[k]
        orr, oi = odd[k]
        if k == 0:
            out[0] = (er + orr, None)
            out[n // 2] = (er - orr, None)
        elif 4 * k == n:
            out[k] = (er, -orr)
        else:
            c, s = math.cos(2 * math.pi * k / n), math.sin(2 * math.pi * k / n)
            if oi is None:
                tr, ti = orr * c, orr * (-s)
            elif 8 * k == n:
                tr, ti = (orr + oi) * c, (oi - orr) * c
            else:
                tr, ti = orr * c + oi * s, oi * c - orr * s
            if ei is None:
                out[k] = (er + tr, ti)
                out[n // 2 - k] = (er - tr, ti)
            else:
                out[k] = (er + tr, ei + ti)
                out[n // 2 - k] = (er - tr, ti - ei)
    return out


def real_ifft(spec):
    n = 2 * (len(spec) - 1)
    if n == 2:
        return [spec[0][0] + spec[1][0], spec[0][0] - spec[1][0]]
    even, odd = [None] * (n // 4 + 1), [None] * (n // 4 + 1)
    for k in range(n // 4 + 1):
        ar, ai = spec[k]
        if k == 0:
            br = spec[n // 2][0]
            even[0] = (ar + br, None)
            odd[0] = (ar - br, None)
        elif 4 * k == n:
            even[k] = (2.0 * ar, None)
            odd[k] = (-2.0 * ai, None)
        else:
            br, bi = spec[n // 2 - k]
            even[k] = (ar + br, ai - bi)
            dr, di = ar - br, ai + bi
            c, s = math.cos(2 * math.pi * k / n), math.sin(2 * math.pi * k / n)
            if 8 * k == n:
                odd[k] = ((dr - di) * c, (dr + di) * c)
            else:
                odd[k] = (dr * c - di * s, dr * s + di * c)
    xe, xo = real_ifft(even), real_ifft(odd)
    out = []
    for a, b in zip(xe, xo):
        out += [a, b]
    return out


def pack_kernel(u_hbm, v_hbm, h_hbm, cut_hbm, speed_hbm, o_ref, cut_ref, speed_ref, raw, tmp, cut, speed, sem):
    copies = [
        pltpu.make_async_copy(src, raw.at[f], sem.at[f])
        for f, src in enumerate((u_hbm, v_hbm, h_hbm))
    ]
    copies.append(pltpu.make_async_copy(cut_hbm, cut, sem.at[3]))
    copies.append(pltpu.make_async_copy(speed_hbm, speed, sem.at[4]))
    for copy in copies:
        copy.start()
    tmp[...] = jnp.zeros_like(tmp)
    inner = lax.broadcasted_iota(jnp.int32, (128, 128), 1) % 64
    extra = None
    for f in (2, 0, 1):
        copies[f].wait()
        for j in range(ROWS):
            tmp[f, j // 2, j % 2 * 64 : j % 2 * 64 + NR, :] = raw[f, :, j, :]
        for half in (1, 0):
            n = 2 * f + half
            turned = tmp[f, half].T
            if n == SLOTS:
                extra = turned
                continue
            if n < 3:
                turned = jnp.where(inner < 48, turned, spare_roll(extra, n))
            for l in range(LV):
                o_ref[:, n, l, :] = turned[l * NB : (l + 1) * NB, :]
    copies[3].wait()
    copies[4].wait()
    z = lax.axis_index("lat")
    p = (lax.axis_index("lon_0") * 4 + lax.axis_index("lon_1")) * 2 + lax.axis_index("lon_2")
    total = cut.shape[0]
    sub = lax.broadcasted_iota(jnp.int32, (16, 128), 0)
    rows = jnp.full((16, 128), -1, jnp.int32)
    for i in range(ROWS + 2 * HALO):
        g = z * ROWS + i - HALO
        inside = jnp.logical_and(g >= 0, g < total)
        rows = jnp.where(sub == i, jnp.where(inside, cut[jnp.clip(g, 0, total - 1)], -1), rows)
    cut_ref[...] = rows
    sub = lax.broadcasted_iota(jnp.int32, (8, 128), 0)
    value = jnp.zeros((8, 128), jnp.float32)
    for l in range(LV):
        value = jnp.where(sub % LV == l, speed[l * NB + p], value)
    speed_ref[...] = value


def spare_roll(a, n):
    return pltpu.roll(a, 48 - 16 * n, 1)


def from_spare(tiles, inner):
    one, two, three = (pltpu.roll(t, 128 - 48 + 16 * n, 1) for n, t in enumerate(tiles))
    return jnp.where(inner < 16, one, jnp.where(inner < 32, two, three))


def split_store(ref, at, re, im):
    x = jnp.concatenate([re, im], axis=0)
    high = x.astype(jnp.bfloat16)
    rest = x - high.astype(jnp.float32)
    mid = rest.astype(jnp.bfloat16)
    low = (rest - mid.astype(jnp.float32)).astype(jnp.bfloat16)
    for i, part in enumerate((high, mid, high, mid, high, low)):
        ref[at, i * 128 : (i + 1) * 128] = part


def swap_sub(a, b, low):
    return jnp.where(low, a, pltpu.roll(b, 4, 0)), jnp.where(low, pltpu.roll(a, 4, 0), b)


def swap_lane(a, b, low):
    return jnp.where(low, a, pltpu.roll(b, 64, 1)), jnp.where(low, pltpu.roll(a, 64, 1), b)


def halves():
    sub = lax.broadcasted_iota(jnp.int32, (8, 128), 0) < 4
    lane = lax.broadcasted_iota(jnp.int32, (8, 128), 1)
    return sub, lane < 64, lane % 64


def forward_kernel(z_ref, dft_ref, tw_ref, own_ref, one_ref, two_ref, x_ref, y_ref):
    even = lax.axis_index("lon_2") == 0
    sub, lane, inner = halves()
    inner4 = lax.broadcasted_iota(jnp.int32, (LV, 128), 1) % 64

    def slot(d, n):
        if n < SLOTS:
            return z_ref[d, n]
        return from_spare([z_ref[d, i] for i in range(3)], inner4)

    for f in range(3):
        spec = real_fft(
            [jnp.concatenate([slot(d, 2 * f), slot(d, 2 * f + 1)], axis=0) for d in range(NB)]
        )
        for k in range(NK):
            a, b = spec[k]
            c, s = tw_ref[k, 0:1, :], tw_ref[k, 1:2, :]
            if b is None:
                re, im = a * c, -(a * s)
            else:
                re, im = a * c + b * s, b * c - a * s
            split_store(x_ref, slice((f * NK + k) * 16, (f * NK + k) * 16 + 16), re, im)
    y_ref[...] = jnp.dot(x_ref[...], dft_ref[...], preferred_element_type=jnp.float32)
    for i in range(PAIRS):
        tiles = []
        for f in range(3):
            parts = []
            for k in (2 * i, 2 * i + 1):
                if k == NK:
                    parts.append((jnp.zeros((8, 128), jnp.float32),) * 2)
                    continue
                at = (f * NK + k) * 16
                re = y_ref[at : at + 8, :128] + y_ref[at + 8 : at + 16, 128:]
                im = y_ref[at + 8 : at + 16, :128] - y_ref[at : at + 8, 128:]
                parts.append(swap_sub(re, im, sub))
            rows = []
            for half in range(2):
                rows += swap_lane(parts[0][half], parts[1][half], lane)
            for j in range(ROWS):
                own_ref[(i * 3 + f) * ROWS + j] = rows[j]
            tiles.append(rows)
        u, v, h = tiles
        edges = []
        for first in (1, 0):
            main = v[first : first + 3] + h[first : first + 3]
            side = u[2:4] if first else u[0:2]
            edges.append(
                [jnp.where(inner < 48, main[n], spare_roll(side[n // 3], n % 3)) for n in range(6)]
            )
        for n, (south, north) in enumerate(zip(*edges)):
            one_ref[i * 6 + n] = jnp.where(even, south, north)
            two_ref[i * 6 + n] = jnp.where(even, north, south)


def step_kernel(
    own_ref, one_ref, two_ref, cut_ref, speed_ref, slope_ref, least_ref, band_ref, dft_ref, tw_ref,
    w_ref, x_ref, y_ref, hold_ref,
):
    z = lax.axis_index("lat")
    even = lax.axis_index("lon_2") == 0
    sub, lane, inner = halves()
    speed = speed_ref[...]
    turn_speed = jnp.where(sub, -speed, speed)
    half_speed = 0.5 * speed

    def body(i, carry):
        def received(a_ref, b_ref):
            tiles = [jnp.where(even, a_ref[i * 6 + n], b_ref[i * 6 + n]) for n in range(6)]
            side = [from_spare(tiles[n : n + 3], inner) for n in (0, 3)]
            return side, tiles[:3], tiles[3:]

        above, below = received(one_ref, two_ref), received(two_ref, one_ref)
        mine = [[own_ref[(i * 3 + f) * ROWS + j] for j in range(ROWS)] for f in range(3)]
        u = [None] + above[0] + mine[0] + below[0] + [None]
        v = above[1] + mine[1] + below[1]
        h = above[2] + mine[2] + below[2]
        start = (u, v, h)
        least = least_ref[i]
        wave = turn_speed * slope_ref[i]
        count = ROWS + 2 * HALO
        keep, zs = [None] * count, [None] * count
        for j in range(1, count - 1):
            keep[j] = jnp.where(least <= cut_ref[j : j + 1, :], 1.0, 0.0)
            zs[j] = wave * band_ref[z, 1, j : j + 1, :]

        def advance(state, margin, scale):
            su, sv, sh = state
            vc = [None] * count
            for j in range(margin - 1, count - margin + 1):
                vc[j] = sv[j] * band_ref[z, 2, j : j + 1, :]
            out = ([None] * count, [None] * count, [None] * count)
            for j in range(margin, count - margin):
                cor = band_ref[z, 0, j : j + 1, :]
                tu = cor * sv[j] - zs[j] * pltpu.roll(sh[j], 4, 0)
                tv = cor * su[j] + half_speed * (sh[j - 1] - sh[j + 1])
                th = zs[j] * pltpu.roll(su[j], 4, 0) + (speed * band_ref[z, 3, j : j + 1, :]) * (
                    vc[j - 1] - vc[j + 1]
                )
                if scale is None:
                    out[0][j], out[1][j], out[2][j] = keep[j] * tu, -keep[j] * tv, -keep[j] * th
                else:
                    m = keep[j] * scale
                    out[0][j] = u[j] + m * tu
                    out[1][j] = v[j] - m * tv
                    out[2][j] = h[j] - m * th
            return out

        gain = advance(advance(advance(start, 1, 1.0 / 3.0), 2, 0.5), 3, None)
        for f in range(3):
            rows = gain[f][HALO : HALO + ROWS]
            north, south = swap_lane(rows[0], rows[1], lane), swap_lane(rows[2], rows[3], lane)
            for side in range(2):
                re, im = swap_sub(north[side], south[side], sub)
                at = (f * 2 * PAIRS + side) * 16 + i * 32
                split_store(x_ref, pl.ds(at, 16), re, im)
        return carry

    for i in range(PAIRS):
        body(i, 0)
    y_ref[...] = jnp.dot(x_ref[...], dft_ref[...], preferred_element_type=jnp.float32)
    for f in (2, 0, 1):
        spec = []
        for k in range(NK):
            at = (f * 2 * PAIRS + k) * 16
            a = y_ref[at : at + 8, :128] - y_ref[at + 8 : at + 16, 128:]
            b = y_ref[at + 8 : at + 16, :128] + y_ref[at : at + 8, 128:]
            c, s = tw_ref[k, 0:1, :], tw_ref[k, 1:2, :]
            spec.append((a * c - b * s, a * s + b * c))
        for d, value in enumerate(real_ifft(spec)):
            if f == 2:
                w_ref[d, 4] = value[:LV]
                low = pltpu.roll(value, LV, 0)
                hold_ref[d] = jnp.where(sub, low, value)
                continue
            extra = hold_ref[d]
            if f == 0:
                extra = jnp.where(sub, spare_roll(extra, 0), spare_roll(extra, 1))
                value = jnp.where(inner < 48, value, extra)
            else:
                extra = spare_roll(extra, 2)
                value = jnp.where(jnp.logical_and(sub, inner >= 48), extra, value)
            w_ref[d, 2 * f] = value[:LV]
            w_ref[d, 2 * f + 1] = value[LV:]


def unpack_kernel(w_ref, u_ref, v_ref, h_ref, u_hbm, v_hbm, h_hbm, out, sem):
    copies = []
    inner = lax.broadcasted_iota(jnp.int32, (128, 128), 1) % 64

    def slot(n):
        if n == SLOTS:
            return from_spare([slot(i) for i in range(3)], inner)
        return jnp.concatenate([w_ref[:, n, l, :] for l in range(LV)], axis=0)

    for f, (ref, hbm) in enumerate(((u_ref, u_hbm), (v_ref, v_hbm), (h_ref, h_hbm))):
        for half in range(2):
            turned = slot(2 * f + half).T
            for side in range(2):
                j = half * 2 + side
                out[f, :, j, :] = ref[:, j, :] + turned[side * 64 : side * 64 + NR, :]
        copies.append(pltpu.make_async_copy(out.at[f], hbm, sem.at[f]))
        copies[-1].start()
    for copy in copies:
        copy.wait()


def vmem(count):
    return [pl.BlockSpec(memory_space=pltpu.VMEM)] * count


def hbm(count):
    return [pl.BlockSpec(memory_space=pltpu.HBM)] * count


def shaped(*dims):
    return jax.ShapeDtypeStruct(dims, jnp.float32)


def shards(u_wind, v_wind, height, wave_speed, cutoff):
    bands = lax.axis_size("lat")
    dft, twid, twid_back, slope, least, per_band = host_tables(bands)
    levels = u_wind.shape[2]
    packed, cut_rows, speeds = pl.pallas_call(
        pack_kernel,
        out_shape=(
            shaped(NB, SLOTS, LV, 128),
            jax.ShapeDtypeStruct((16, 128), jnp.int32),
            shaped(8, 128),
        ),
        in_specs=hbm(5),
        out_specs=tuple(vmem(3)),
        scratch_shapes=[
            pltpu.VMEM((3, NR, ROWS, levels), jnp.float32),
            pltpu.VMEM((3, 2, 128, levels), jnp.float32),
            pltpu.SMEM(cutoff.shape, jnp.int32),
            pltpu.SMEM(wave_speed.shape, jnp.float32),
            pltpu.SemaphoreType.DMA((5,)),
        ],
        name="pack",
        compiler_params=PARAMS,
    )(*(pltpu.with_memory_space_constraint(a, pltpu.HBM) for a in (u_wind, v_wind, height, cutoff, wave_speed)))
    circles = lax.all_to_all(packed, LON, 0, 0, tiled=True)
    own, one, two = pl.pallas_call(
        forward_kernel,
        out_shape=(
            shaped(PAIRS * 3 * ROWS, 8, 128),
            shaped(PAIRS * 6, 8, 128),
            shaped(PAIRS * 6, 8, 128),
        ),
        in_specs=vmem(3),
        out_specs=tuple(vmem(3)),
        scratch_shapes=[
            pltpu.VMEM((3 * NK * 16, 768), jnp.bfloat16),
            pltpu.VMEM((3 * NK * 16, 256), jnp.float32),
        ],
        name="forward",
        compiler_params=PARAMS,
    )(circles, dft, twid)
    stop = bands - 1
    south = [[(2 * i + c, 2 * i + 2 + c) for i in range(stop)] for c in range(2)]
    north = [[(b, a) for a, b in pairs] for pairs in south]
    one = lax.ppermute(one, ("lat", "lon_2"), south[0] + north[1])
    two = lax.ppermute(two, ("lat", "lon_2"), north[0] + south[1])
    waves = pl.pallas_call(
        step_kernel,
        out_shape=shaped(NB, SLOTS, LV, 128),
        in_specs=vmem(10),
        out_specs=vmem(1)[0],
        scratch_shapes=[
            pltpu.VMEM((3 * 2 * PAIRS * 16, 768), jnp.bfloat16),
            pltpu.VMEM((3 * 2 * PAIRS * 16, 256), jnp.float32),
            pltpu.VMEM((NB, 2 * LV, 128), jnp.float32),
        ],
        name="sections",
        compiler_params=PARAMS,
    )(own, one, two, cut_rows, speeds, slope, least, per_band, dft, twid_back)
    waves = lax.all_to_all(waves, LON, 0, 0, tiled=True)
    return pl.pallas_call(
        unpack_kernel,
        out_shape=tuple(shaped(NR, ROWS, levels) for _ in range(3)),
        in_specs=vmem(4),
        out_specs=tuple(hbm(3)),
        scratch_shapes=[
            pltpu.VMEM((3, NR, ROWS, levels), jnp.float32),
            pltpu.SemaphoreType.DMA((3,)),
        ],
        name="unpack",
        compiler_params=PARAMS,
    )(waves, u_wind, v_wind, height)


def solution(mesh):
    split = Mesh(
        mesh.devices.reshape(mesh.shape["lat"], 4, 4, 2), ("lat", "lon_0", "lon_1", "lon_2")
    )
    return jax.shard_map(
        shards,
        mesh=split,
        in_specs=(P(LON, "lat", None), P(LON, "lat", None), P(LON, "lat", None), P(), P()),
        out_specs=(P(LON, "lat", None), P(LON, "lat", None), P(LON, "lat", None)),
        check_vma=False,
    )
```

```python
import math

import jax
import jax.numpy as jnp
import ml_dtypes
import numpy as np
from jax import lax
from jax.experimental import pallas as pl
from jax.experimental.pallas import tpu as pltpu
from jax.sharding import Mesh
from jax.sharding import PartitionSpec as P

LON = ("lon_0", "lon_1", "lon_2")

NB = 32
NR = 45
PTS = NB * NR
NK = NB // 2 + 1
PAIRS = (NK + 1) // 2
ROWS = 4
HALO = 3
LV = 4
SLOTS = 5
SENT = 41
FAR = 1 << 20
PARAMS = pltpu.CompilerParams(vmem_limit_bytes=12 << 20)


def split_three(a):
    high = a.astype(ml_dtypes.bfloat16)
    rest = a - high.astype(np.float64)
    mid = rest.astype(ml_dtypes.bfloat16)
    low = (rest - mid.astype(np.float64)).astype(ml_dtypes.bfloat16)
    return high, mid, low


def host_tables(bands):
    r = np.arange(NR)
    ang = 2.0 * np.pi * np.outer(r, r) / NR
    dft = np.zeros((128, 256))
    twid = np.zeros((NK, 2, 128))
    for side in range(2):
        at = slice(side * 64, side * 64 + NR)
        dft[at, at] = np.cos(ang)
        dft[at, 128 + side * 64 : 128 + side * 64 + NR] = np.sin(ang)
        for k in range(NK):
            twid[k, 0, at] = np.cos(2.0 * np.pi * k * r / PTS)
            twid[k, 1, at] = np.sin(2.0 * np.pi * k * r / PTS)
    high, mid, low = split_three(dft)
    dft = np.concatenate([high, high, mid, mid, low, high], axis=0)
    lane = np.arange(128)
    k1 = 2 * np.arange(PAIRS)[:, None] + lane[None, :] // 64
    wav = k1 + NB * (lane % 64)[None, :]
    ok = (k1 < NK) & (lane % 64 < NR)[None, :]
    slope = np.where(ok, np.sin(2.0 * np.pi * wav / PTS), 0.0)
    least = np.where(ok, np.minimum(wav, PTS - wav), FAR)
    total = bands * ROWS
    per_band = np.zeros((bands, 4, 16, 128), np.float32)
    row = np.arange(-HALO, ROWS + HALO)
    half_pi = np.float32(0.5 * math.pi)
    for z in range(bands):
        g = z * ROWS + row
        ok = (g >= 0) & (g < total)
        lat = half_pi - (g.astype(np.float32) + np.float32(0.5)) * np.float32(math.pi / total)
        cos = np.where(ok, np.cos(lat, dtype=np.float32), np.float32(1.0))
        sin = np.sin(lat, dtype=np.float32)
        rows = (0.25 * sin, PTS / (2.0 * total) / cos, cos, 0.5 / cos)
        for c, value in enumerate(rows):
            per_band[z, c, : len(row), :] = np.where(ok, value, 0.0)[:, None]
    f32 = lambda a: jnp.asarray(np.asarray(a, np.float32))
    return (
        jnp.asarray(dft),
        f32(twid),
        f32(twid / PTS),
        f32(slope[:, None, :]),
        jnp.asarray(least[:, None, :].astype(np.int32)),
        f32(per_band),
    )


def real_fft(xs):
    n = len(xs)
    if n == 1:
        return [(xs[0], None)]
    even, odd = real_fft(xs[0::2]), real_fft(xs[1::2])
    out = [None] * (n // 2 + 1)
    for k in range(n // 4 + 1 if n > 2 else 1):
        er, ei = even[k]
        orr, oi = odd[k]
        if k == 0:
            out[0] = (er + orr, None)
            out[n // 2] = (er - orr, None)
        elif 4 * k == n:
            out[k] = (er, -orr)
        else:
            c, s = math.cos(2 * math.pi * k / n), math.sin(2 * math.pi * k / n)
            if oi is None:
                tr, ti = orr * c, orr * (-s)
            elif 8 * k == n:
                tr, ti = (orr + oi) * c, (oi - orr) * c
            else:
                tr, ti = orr * c + oi * s, oi * c - orr * s
            if ei is None:
                out[k] = (er + tr, ti)
                out[n // 2 - k] = (er - tr, ti)
            else:
                out[k] = (er + tr, ei + ti)
                out[n // 2 - k] = (er - tr, ti - ei)
    return out


def real_ifft(spec):
    n = 2 * (len(spec) - 1)
    if n == 2:
        return [spec[0][0] + spec[1][0], spec[0][0] - spec[1][0]]
    even, odd = [None] * (n // 4 + 1), [None] * (n // 4 + 1)
    for k in range(n // 4 + 1):
        ar, ai = spec[k]
        if k == 0:
            br = spec[n // 2][0]
            even[0] = (ar + br, None)
            odd[0] = (ar - br, None)
        elif 4 * k == n:
            even[k] = (2.0 * ar, None)
            odd[k] = (-2.0 * ai, None)
        else:
            br, bi = spec[n // 2 - k]
            even[k] = (ar + br, ai - bi)
            dr, di = ar - br, ai + bi
            c, s = math.cos(2 * math.pi * k / n), math.sin(2 * math.pi * k / n)
            if 8 * k == n:
                odd[k] = ((dr - di) * c, (dr + di) * c)
            else:
                odd[k] = (dr * c - di * s, dr * s + di * c)
    xe, xo = real_ifft(even), real_ifft(odd)
    out = []
    for a, b in zip(xe, xo):
        out += [a, b]
    return out


def pack_kernel(u_hbm, v_hbm, h_hbm, cut_hbm, speed_hbm, o_ref, cut_ref, speed_ref, raw, tmp, cut, speed, sem):
    fields = [
        pltpu.make_async_copy(src, raw.at[f], sem.at[f])
        for f, src in ((2, h_hbm), (0, u_hbm), (1, v_hbm))
    ]
    small = [
        pltpu.make_async_copy(cut_hbm, cut, sem.at[3]),
        pltpu.make_async_copy(speed_hbm, speed, sem.at[4]),
    ]
    for copy in fields + small:
        copy.start()
    tmp[...] = jnp.zeros_like(tmp)
    inner = lax.broadcasted_iota(jnp.int32, (128, 128), 1) % 64
    extra = None
    for f, copy in zip((2, 0, 1), fields):
        copy.wait()
        for j in range(ROWS):
            tmp[f, j // 2, j % 2 * 64 : j % 2 * 64 + NR, :] = raw[f, :, j, :]
        for half in (1, 0):
            n = 2 * f + half
            turned = tmp[f, half].T
            if n == SLOTS:
                extra = turned
                continue
            if n < 3:
                turned = jnp.where(inner < 48, turned, spare_roll(extra, n))
            for l in range(LV):
                o_ref[:, n, l, :] = turned[l * NB : (l + 1) * NB, :]
    for copy in small:
        copy.wait()
    z = lax.axis_index("lat")
    p = (lax.axis_index("lon_0") * 4 + lax.axis_index("lon_1")) * 2 + lax.axis_index("lon_2")
    total = cut.shape[0]
    sub = lax.broadcasted_iota(jnp.int32, (16, 128), 0)
    rows = jnp.full((16, 128), -1, jnp.int32)
    for i in range(ROWS + 2 * HALO):
        g = z * ROWS + i - HALO
        inside = jnp.logical_and(g >= 0, g < total)
        rows = jnp.where(sub == i, jnp.where(inside, cut[jnp.clip(g, 0, total - 1)], -1), rows)
    cut_ref[...] = rows
    sub = lax.broadcasted_iota(jnp.int32, (8, 128), 0)
    value = jnp.zeros((8, 128), jnp.float32)
    for l in range(LV):
        value = jnp.where(sub % LV == l, speed[l * NB + p], value)
    speed_ref[...] = value


def spare_roll(a, n):
    return pltpu.roll(a, 48 - 16 * n, 1)


def from_spare(tiles, inner):
    one, two, three = (pltpu.roll(t, 128 - 48 + 16 * n, 1) for n, t in enumerate(tiles))
    return jnp.where(inner < 16, one, jnp.where(inner < 32, two, three))


def split_store(ref, at, re, im):
    x = jnp.concatenate([re, im], axis=0)
    high = x.astype(jnp.bfloat16)
    rest = x - high.astype(jnp.float32)
    mid = rest.astype(jnp.bfloat16)
    low = (rest - mid.astype(jnp.float32)).astype(jnp.bfloat16)
    for i, part in enumerate((high, mid, high, mid, high, low)):
        ref[at, i * 128 : (i + 1) * 128] = part


def swap_sub(a, b, low):
    return jnp.where(low, a, pltpu.roll(b, 4, 0)), jnp.where(low, pltpu.roll(a, 4, 0), b)


def swap_lane(a, b, low):
    return jnp.where(low, a, pltpu.roll(b, 64, 1)), jnp.where(low, pltpu.roll(a, 64, 1), b)


def halves():
    sub = lax.broadcasted_iota(jnp.int32, (8, 128), 0) < 4
    lane = lax.broadcasted_iota(jnp.int32, (8, 128), 1)
    return sub, lane < 64, lane % 64


class Rows:
    def __init__(self, z, i, cut_ref, speed, turn_speed, slope_ref, least_ref, band_ref):
        self.z, self.cut, self.band, self.speed = z, cut_ref, band_ref, speed
        self.least, self.wave = least_ref[i], turn_speed * slope_ref[i]

    def of(self, c, row):
        return self.band[self.z, c, row + HALO : row + HALO + 1, :]

    def keep(self, row):
        kept = self.least <= self.cut[row + HALO : row + HALO + 1, :]
        return jnp.where(kept, 1.0, 0.0)

    def cor(self, row):
        return self.of(0, row)

    def zonal(self, row):
        return self.wave * self.of(1, row)

    def cos(self, row):
        return self.of(2, row)

    def merid(self, row):
        return self.speed * self.of(3, row)


def swap_parts(a):
    return pltpu.roll(a, LV, 0)


def edge_sums(u, v, h, rows, half_speed, edge, step):
    near, far = edge + step, edge + 2 * step
    sign = -1.0 if step > 0 else 1.0
    keep, cor, zonal = rows.keep(edge), rows.cor(edge), rows.zonal(edge)
    third, half = keep * (1.0 / 3.0), keep * 0.5
    hs, merid = sign * half_speed, sign * rows.merid(edge)
    vc_edge, vc_near, vc_far = (v[j] * rows.cos(j) for j in (edge, near, far))
    v1 = v[edge] - third * (cor * u[edge] + hs * h[near])
    h1 = h[edge] - third * (zonal * swap_parts(u[edge]) + merid * vc_near)
    u1 = u[edge] + third * (cor * v[edge] - zonal * swap_parts(h[edge]))
    near_third = rows.keep(near) * (1.0 / 3.0)
    near_v1 = v[near] - near_third * (rows.cor(near) * u[near] + hs * (h[far] - h[edge]))
    near_h1 = h[near] - near_third * (
        rows.zonal(near) * swap_parts(u[near]) + sign * rows.merid(near) * (vc_far - vc_edge)
    )
    v2 = v[edge] - half * (cor * u1 + hs * near_h1)
    h2 = h[edge] - half * (zonal * swap_parts(u1) + merid * (near_v1 * rows.cos(near)))
    return [v[edge], h[edge], v1, h1, v2, h2]


def field_dot(y_ref, x_ref, dft_ref, f, count):
    at = slice(f * count * 16, (f + 1) * count * 16)
    y_ref[at, :] = jnp.dot(x_ref[at, :], dft_ref[...], preferred_element_type=jnp.float32)


def forward_kernel(
    z_ref, dft_ref, tw_ref, cut_ref, speed_ref, slope_ref, least_ref, band_ref,
    own_ref, one_ref, two_ref, x_ref, y_ref,
):
    z = lax.axis_index("lat")
    even = lax.axis_index("lon_2") == 0
    sub, lane, inner = halves()
    inner4 = lax.broadcasted_iota(jnp.int32, (LV, 128), 1) % 64

    def slot(d, n):
        if n < SLOTS:
            return z_ref[d, n]
        return from_spare([z_ref[d, i] for i in range(3)], inner4)

    for f in range(3):
        spec = real_fft(
            [jnp.concatenate([slot(d, 2 * f), slot(d, 2 * f + 1)], axis=0) for d in range(NB)]
        )
        for k in range(NK):
            a, b = spec[k]
            c, s = tw_ref[k, 0:1, :], tw_ref[k, 1:2, :]
            if b is None:
                re, im = a * c, -(a * s)
            else:
                re, im = a * c + b * s, b * c - a * s
            split_store(x_ref, slice((f * NK + k) * 16, (f * NK + k) * 16 + 16), re, im)
        field_dot(y_ref, x_ref, dft_ref, f, NK)
    speed = speed_ref[...]
    turn_speed = jnp.where(sub, -speed, speed)
    half_speed = 0.5 * speed
    spare = {}
    for i in reversed(range(PAIRS)):
        tiles = []
        for f in range(3):
            parts = []
            for k in (2 * i, 2 * i + 1):
                if k == NK:
                    parts.append((jnp.zeros((8, 128), jnp.float32),) * 2)
                    continue
                at = (f * NK + k) * 16
                re = y_ref[at : at + 8, :128] + y_ref[at + 8 : at + 16, 128:]
                im = y_ref[at + 8 : at + 16, :128] - y_ref[at : at + 8, 128:]
                parts.append(swap_sub(re, im, sub))
            rows = []
            for half in range(2):
                rows += swap_lane(parts[0][half], parts[1][half], lane)
            for j in range(ROWS):
                own_ref[(i * 3 + f) * ROWS + j] = rows[j]
            tiles.append(rows)
        u, v, h = tiles
        rows = Rows(z, i, cut_ref, speed, turn_speed, slope_ref, least_ref, band_ref)
        to_south = edge_sums(u, v, h, rows, half_speed, ROWS - 1, -1)
        to_north = edge_sums(u, v, h, rows, half_speed, 0, 1)
        for n, (south, north) in enumerate(zip(to_south, to_north)):
            t = i * 6 + n
            for ref, tile in (
                (one_ref, jnp.where(even, south, north)),
                (two_ref, jnp.where(even, north, south)),
            ):
                if t >= SENT:
                    spare[ref is one_ref, t - SENT] = tile
                elif t < 3 * (PAIRS * 6 - SENT):
                    extra = spare_roll(spare[ref is one_ref, t // 3], t % 3)
                    ref[t] = jnp.where(inner < 48, tile, extra)
                else:
                    ref[t] = tile


def step_kernel(
    own_ref, one_ref, two_ref, cut_ref, speed_ref, slope_ref, least_ref, band_ref, dft_ref, tw_ref,
    w_ref, x_ref, y_ref, hold_ref,
):
    z = lax.axis_index("lat")
    even = lax.axis_index("lon_2") == 0
    sub, lane, inner = halves()
    speed = speed_ref[...]
    turn_speed = jnp.where(sub, -speed, speed)
    half_speed = 0.5 * speed

    def received(a_ref, b_ref, i):
        pick = lambda t: jnp.where(even, a_ref[t], b_ref[t])
        tiles = []
        for t in range(i * 6, i * 6 + 6):
            e = 3 * (t - SENT)
            tiles.append(pick(t) if t < SENT else from_spare([pick(e + c) for c in range(3)], inner))
        return tiles

    for i in range(PAIRS):
        above, below = received(one_ref, two_ref, i), received(two_ref, one_ref, i)
        u, v, h = ([own_ref[(i * 3 + f) * ROWS + j] for j in range(ROWS)] for f in range(3))
        rows = Rows(z, i, cut_ref, speed, turn_speed, slope_ref, least_ref, band_ref)
        span = range(-1, ROWS + 1)
        keep = {j: rows.keep(j) for j in span}
        zonal = {j: rows.zonal(j) for j in range(ROWS)}

        def advance(state, level, scale):
            su, sv, sh = state[:3]
            sv, sh = {j: sv[j] for j in range(ROWS)}, {j: sh[j] for j in range(ROWS)}
            before, after = above[2 * level : 2 * level + 2], below[2 * level : 2 * level + 2]
            if level == 0:
                (sv[-1], sh[-1]), (sv[ROWS], sh[ROWS]) = before, after
            else:
                last = ROWS - 1
                top, end = keep[-1] * state[3], keep[ROWS] * state[3]
                pv, ph = state[4]
                sv[-1] = before[0] + top * half_speed * ph[0]
                sh[-1] = before[1] + top * rows.merid(-1) * (pv[0] * rows.cos(0))
                sv[ROWS] = after[0] - end * half_speed * ph[last]
                sh[ROWS] = after[1] - end * rows.merid(ROWS) * (pv[last] * rows.cos(last))
            vc = {j: sv[j] * rows.cos(j) for j in span}
            out = [], [], []
            for j in range(ROWS):
                cor = rows.cor(j)
                tu = cor * sv[j] - zonal[j] * swap_parts(sh[j])
                tv = cor * su[j] + half_speed * (sh[j - 1] - sh[j + 1])
                th = zonal[j] * swap_parts(su[j]) + rows.merid(j) * (vc[j - 1] - vc[j + 1])
                if scale is None:
                    values = keep[j] * tu, -keep[j] * tv, -keep[j] * th
                else:
                    m = keep[j] * scale
                    values = u[j] + m * tu, v[j] - m * tv, h[j] - m * th
                for into, value in zip(out, values):
                    into.append(value)
            return *out, scale, (sv, sh)

        gain = advance((u, v, h), 0, 1.0 / 3.0)
        gain = advance(gain, 1, 0.5)
        gain = advance(gain, 2, None)
        for f in range(3):
            r = gain[f]
            north, south = swap_lane(r[0], r[1], lane), swap_lane(r[2], r[3], lane)
            for side in range(2):
                re, im = swap_sub(north[side], south[side], sub)
                at = (f * 2 * PAIRS + side) * 16 + i * 32
                split_store(x_ref, pl.ds(at, 16), re, im)
    for f in (2, 0, 1):
        field_dot(y_ref, x_ref, dft_ref, f, 2 * PAIRS)
        spec = []
        for k in range(NK):
            at = (f * 2 * PAIRS + k) * 16
            a = y_ref[at : at + 8, :128] - y_ref[at + 8 : at + 16, 128:]
            b = y_ref[at + 8 : at + 16, :128] + y_ref[at : at + 8, 128:]
            c, s = tw_ref[k, 0:1, :], tw_ref[k, 1:2, :]
            spec.append((a * c - b * s, a * s + b * c))
        for d, value in enumerate(real_ifft(spec)):
            if f == 2:
                w_ref[d, 4] = value[:LV]
                low = pltpu.roll(value, LV, 0)
                hold_ref[d] = jnp.where(sub, low, value)
                continue
            extra = hold_ref[d]
            if f == 0:
                extra = jnp.where(sub, spare_roll(extra, 0), spare_roll(extra, 1))
                value = jnp.where(inner < 48, value, extra)
            else:
                extra = spare_roll(extra, 2)
                value = jnp.where(jnp.logical_and(sub, inner >= 48), extra, value)
            w_ref[d, 2 * f] = value[:LV]
            w_ref[d, 2 * f + 1] = value[LV:]


def unpack_kernel(w_ref, u_ref, v_ref, h_ref, u_hbm, v_hbm, h_hbm, out, sem):
    copies = []
    inner = lax.broadcasted_iota(jnp.int32, (128, 128), 1) % 64

    def slot(n):
        if n == SLOTS:
            return from_spare([slot(i) for i in range(3)], inner)
        return jnp.concatenate([w_ref[:, n, l, :] for l in range(LV)], axis=0)

    for f, (ref, hbm) in enumerate(((u_ref, u_hbm), (v_ref, v_hbm), (h_ref, h_hbm))):
        for half in range(2):
            turned = slot(2 * f + half).T
            for side in range(2):
                j = half * 2 + side
                out[f, :, j, :] = ref[:, j, :] + turned[side * 64 : side * 64 + NR, :]
        copies.append(pltpu.make_async_copy(out.at[f], hbm, sem.at[f]))
        copies[-1].start()
    for copy in copies:
        copy.wait()


def vmem(count):
    return [pl.BlockSpec(memory_space=pltpu.VMEM)] * count


def hbm(count):
    return [pl.BlockSpec(memory_space=pltpu.HBM)] * count


def shaped(*dims):
    return jax.ShapeDtypeStruct(dims, jnp.float32)


def shards(u_wind, v_wind, height, wave_speed, cutoff):
    bands = lax.axis_size("lat")
    dft, twid, twid_back, slope, least, per_band = host_tables(bands)
    levels = u_wind.shape[2]
    packed, cut_rows, speeds = pl.pallas_call(
        pack_kernel,
        out_shape=(
            shaped(NB, SLOTS, LV, 128),
            jax.ShapeDtypeStruct((16, 128), jnp.int32),
            shaped(8, 128),
        ),
        in_specs=hbm(5),
        out_specs=tuple(vmem(3)),
        scratch_shapes=[
            pltpu.VMEM((3, NR, ROWS, levels), jnp.float32),
            pltpu.VMEM((3, 2, 128, levels), jnp.float32),
            pltpu.SMEM(cutoff.shape, jnp.int32),
            pltpu.SMEM(wave_speed.shape, jnp.float32),
            pltpu.SemaphoreType.DMA((5,)),
        ],
        name="pack",
        compiler_params=PARAMS,
    )(*(pltpu.with_memory_space_constraint(a, pltpu.HBM) for a in (u_wind, v_wind, height, cutoff, wave_speed)))
    circles = lax.all_to_all(packed, LON, 0, 0, tiled=True)
    own, one, two = pl.pallas_call(
        forward_kernel,
        out_shape=(
            shaped(PAIRS * 3 * ROWS, 8, 128),
            shaped(SENT, 8, 128),
            shaped(SENT, 8, 128),
        ),
        in_specs=vmem(8),
        out_specs=tuple(vmem(3)),
        scratch_shapes=[
            pltpu.VMEM((3 * NK * 16, 768), jnp.bfloat16),
            pltpu.VMEM((3 * NK * 16, 256), jnp.float32),
        ],
        name="forward",
        compiler_params=PARAMS,
    )(circles, dft, twid, cut_rows, speeds, slope, least, per_band)
    stop = bands - 1
    south = [[(2 * i + c, 2 * i + 2 + c) for i in range(stop)] for c in range(2)]
    north = [[(b, a) for a, b in pairs] for pairs in south]
    one = lax.ppermute(one, ("lat", "lon_2"), south[0] + north[1])
    two = lax.ppermute(two, ("lat", "lon_2"), north[0] + south[1])
    waves = pl.pallas_call(
        step_kernel,
        out_shape=shaped(NB, SLOTS, LV, 128),
        in_specs=vmem(10),
        out_specs=vmem(1)[0],
        scratch_shapes=[
            pltpu.VMEM((3 * 2 * PAIRS * 16, 768), jnp.bfloat16),
            pltpu.VMEM((3 * 2 * PAIRS * 16, 256), jnp.float32),
            pltpu.VMEM((NB, 2 * LV, 128), jnp.float32),
        ],
        name="sections",
        compiler_params=PARAMS,
    )(own, one, two, cut_rows, speeds, slope, least, per_band, dft, twid_back)
    waves = lax.all_to_all(waves, LON, 0, 0, tiled=True)
    return pl.pallas_call(
        unpack_kernel,
        out_shape=tuple(shaped(NR, ROWS, levels) for _ in range(3)),
        in_specs=vmem(4),
        out_specs=tuple(hbm(3)),
        scratch_shapes=[
            pltpu.VMEM((3, NR, ROWS, levels), jnp.float32),
            pltpu.SemaphoreType.DMA((3,)),
        ],
        name="unpack",
        compiler_params=PARAMS,
    )(waves, u_wind, v_wind, height)


def solution(mesh):
    split = Mesh(
        mesh.devices.reshape(mesh.shape["lat"], 4, 4, 2), ("lat", "lon_0", "lon_1", "lon_2")
    )
    return jax.shard_map(
        shards,
        mesh=split,
        in_specs=(P(LON, "lat", None), P(LON, "lat", None), P(LON, "lat", None), P(), P()),
        out_specs=(P(LON, "lat", None), P(LON, "lat", None), P(LON, "lat", None)),
        check_vma=False,
    )
```

```python
import math

import jax
import jax.numpy as jnp
import ml_dtypes
import numpy as np
from jax import lax
from jax.experimental import pallas as pl
from jax.experimental.pallas import tpu as pltpu
from jax.sharding import Mesh
from jax.sharding import PartitionSpec as P

LON = ("lon_0", "lon_1", "lon_2")

NB = 32
NR = 45
PTS = NB * NR
NK = NB // 2 + 1
PAIRS = (NK + 1) // 2
ROWS = 4
HALO = 3
LV = 4
SLOTS = 5
SENT = 41
FAR = 1 << 20
PARAMS = pltpu.CompilerParams(vmem_limit_bytes=12 << 20)


def split_three(a):
    high = a.astype(ml_dtypes.bfloat16)
    rest = a - high.astype(np.float64)
    mid = rest.astype(ml_dtypes.bfloat16)
    low = (rest - mid.astype(np.float64)).astype(ml_dtypes.bfloat16)
    return high, mid, low


def host_tables(bands):
    r = np.arange(NR)
    ang = 2.0 * np.pi * np.outer(r, r) / NR
    dft = np.zeros((128, 256))
    twid = np.zeros((NK, 2, 128))
    for side in range(2):
        at = slice(side * 64, side * 64 + NR)
        dft[at, at] = np.cos(ang)
        dft[at, 128 + side * 64 : 128 + side * 64 + NR] = np.sin(ang)
        for k in range(NK):
            twid[k, 0, at] = np.cos(2.0 * np.pi * k * r / PTS)
            twid[k, 1, at] = np.sin(2.0 * np.pi * k * r / PTS)
    high, mid, low = split_three(dft)
    dft = np.concatenate([high, high, mid, mid, low, high], axis=0)
    lane = np.arange(128)
    k1 = 2 * np.arange(PAIRS)[:, None] + lane[None, :] // 64
    wav = k1 + NB * (lane % 64)[None, :]
    ok = (k1 < NK) & (lane % 64 < NR)[None, :]
    slope = np.where(ok, np.sin(2.0 * np.pi * wav / PTS), 0.0)
    least = np.where(ok, np.minimum(wav, PTS - wav), FAR)
    total = bands * ROWS
    per_band = np.zeros((bands, 4, 16, 128), np.float32)
    row = np.arange(-HALO, ROWS + HALO)
    half_pi = np.float32(0.5 * math.pi)
    for z in range(bands):
        g = z * ROWS + row
        ok = (g >= 0) & (g < total)
        lat = half_pi - (g.astype(np.float32) + np.float32(0.5)) * np.float32(math.pi / total)
        cos = np.where(ok, np.cos(lat, dtype=np.float32), np.float32(1.0))
        sin = np.sin(lat, dtype=np.float32)
        rows = (0.25 * sin, PTS / (2.0 * total) / cos, cos, 0.5 / cos)
        for c, value in enumerate(rows):
            per_band[z, c, : len(row), :] = np.where(ok, value, 0.0)[:, None]
    f32 = lambda a: jnp.asarray(np.asarray(a, np.float32))
    return (
        jnp.asarray(dft),
        f32(twid),
        f32(twid / PTS),
        f32(slope[:, None, :]),
        jnp.asarray(least[:, None, :].astype(np.int32)),
        f32(per_band),
    )


def real_fft(xs):
    n = len(xs)
    if n == 1:
        return [(xs[0], None)]
    even, odd = real_fft(xs[0::2]), real_fft(xs[1::2])
    out = [None] * (n // 2 + 1)
    for k in range(n // 4 + 1 if n > 2 else 1):
        er, ei = even[k]
        orr, oi = odd[k]
        if k == 0:
            out[0] = (er + orr, None)
            out[n // 2] = (er - orr, None)
        elif 4 * k == n:
            out[k] = (er, -orr)
        else:
            c, s = math.cos(2 * math.pi * k / n), math.sin(2 * math.pi * k / n)
            if oi is None:
                tr, ti = orr * c, orr * (-s)
            elif 8 * k == n:
                tr, ti = (orr + oi) * c, (oi - orr) * c
            else:
                tr, ti = orr * c + oi * s, oi * c - orr * s
            if ei is None:
                out[k] = (er + tr, ti)
                out[n // 2 - k] = (er - tr, ti)
            else:
                out[k] = (er + tr, ei + ti)
                out[n // 2 - k] = (er - tr, ti - ei)
    return out


def real_ifft(spec):
    n = 2 * (len(spec) - 1)
    if n == 2:
        return [spec[0][0] + spec[1][0], spec[0][0] - spec[1][0]]
    even, odd = [None] * (n // 4 + 1), [None] * (n // 4 + 1)
    for k in range(n // 4 + 1):
        ar, ai = spec[k]
        if k == 0:
            br = spec[n // 2][0]
            even[0] = (ar + br, None)
            odd[0] = (ar - br, None)
        elif 4 * k == n:
            even[k] = (2.0 * ar, None)
            odd[k] = (-2.0 * ai, None)
        else:
            br, bi = spec[n // 2 - k]
            even[k] = (ar + br, ai - bi)
            dr, di = ar - br, ai + bi
            c, s = math.cos(2 * math.pi * k / n), math.sin(2 * math.pi * k / n)
            if 8 * k == n:
                odd[k] = ((dr - di) * c, (dr + di) * c)
            else:
                odd[k] = (dr * c - di * s, dr * s + di * c)
    xe, xo = real_ifft(even), real_ifft(odd)
    out = []
    for a, b in zip(xe, xo):
        out += [a, b]
    return out


def pack_kernel(u_hbm, v_hbm, h_hbm, cut_hbm, speed_hbm, o_ref, cut_ref, speed_ref, raw, tmp, cut, speed, sem):
    fields = [
        pltpu.make_async_copy(src, raw.at[f], sem.at[f])
        for f, src in ((2, h_hbm), (0, u_hbm), (1, v_hbm))
    ]
    small = [
        pltpu.make_async_copy(cut_hbm, cut, sem.at[3]),
        pltpu.make_async_copy(speed_hbm, speed, sem.at[4]),
    ]
    for copy in fields + small:
        copy.start()
    tmp[...] = jnp.zeros_like(tmp)
    inner = lax.broadcasted_iota(jnp.int32, (128, 128), 1) % 64
    extra = None
    for f, copy in zip((2, 0, 1), fields):
        copy.wait()
        for j in range(ROWS):
            tmp[f, j // 2, j % 2 * 64 : j % 2 * 64 + NR, :] = raw[f, :, j, :]
        for half in (1, 0):
            n = 2 * f + half
            turned = tmp[f, half].T
            if n == SLOTS:
                extra = turned
                continue
            if n < 3:
                turned = jnp.where(inner < 48, turned, spare_roll(extra, n))
            for l in range(LV):
                o_ref[:, n, l, :] = turned[l * NB : (l + 1) * NB, :]
    for copy in small:
        copy.wait()
    z = lax.axis_index("lat")
    p = (lax.axis_index("lon_0") * 4 + lax.axis_index("lon_1")) * 2 + lax.axis_index("lon_2")
    total = cut.shape[0]
    sub = lax.broadcasted_iota(jnp.int32, (16, 128), 0)
    rows = jnp.full((16, 128), -1, jnp.int32)
    for i in range(ROWS + 2 * HALO):
        g = z * ROWS + i - HALO
        inside = jnp.logical_and(g >= 0, g < total)
        rows = jnp.where(sub == i, jnp.where(inside, cut[jnp.clip(g, 0, total - 1)], -1), rows)
    cut_ref[...] = rows
    sub = lax.broadcasted_iota(jnp.int32, (8, 128), 0)
    value = jnp.zeros((8, 128), jnp.float32)
    for l in range(LV):
        value = jnp.where(sub % LV == l, speed[l * NB + p], value)
    speed_ref[...] = value


def spare_roll(a, n):
    return pltpu.roll(a, 48 - 16 * n, 1)


def from_spare(tiles, inner):
    one, two, three = (pltpu.roll(t, 128 - 48 + 16 * n, 1) for n, t in enumerate(tiles))
    return jnp.where(inner < 16, one, jnp.where(inner < 32, two, three))


def split_store(ref, at, re, im):
    x = jnp.concatenate([re, im], axis=0)
    high = x.astype(jnp.bfloat16)
    rest = x - high.astype(jnp.float32)
    mid = rest.astype(jnp.bfloat16)
    low = (rest - mid.astype(jnp.float32)).astype(jnp.bfloat16)
    for i, part in enumerate((high, mid, high, mid, high, low)):
        ref[at, i * 128 : (i + 1) * 128] = part


def swap_sub(a, b, low):
    return jnp.where(low, a, pltpu.roll(b, 4, 0)), jnp.where(low, pltpu.roll(a, 4, 0), b)


def swap_lane(a, b, low):
    return jnp.where(low, a, pltpu.roll(b, 64, 1)), jnp.where(low, pltpu.roll(a, 64, 1), b)


def halves():
    sub = lax.broadcasted_iota(jnp.int32, (8, 128), 0) < 4
    lane = lax.broadcasted_iota(jnp.int32, (8, 128), 1)
    return sub, lane < 64, lane % 64


class Rows:
    def __init__(self, z, i, cut_ref, speed, turn_speed, slope_ref, least_ref, band_ref):
        self.z, self.cut, self.band, self.speed = z, cut_ref, band_ref, speed
        self.least, self.wave = least_ref[i], turn_speed * slope_ref[i]

    def of(self, c, row):
        return self.band[self.z, c, row + HALO : row + HALO + 1, :]

    def keep(self, row):
        kept = self.least <= self.cut[row + HALO : row + HALO + 1, :]
        return jnp.where(kept, 1.0, 0.0)

    def cor(self, row):
        return self.of(0, row)

    def zonal(self, row):
        return self.wave * self.of(1, row)

    def cos(self, row):
        return self.of(2, row)

    def merid(self, row):
        return self.speed * self.of(3, row)


def swap_parts(a):
    return pltpu.roll(a, LV, 0)


def edge_sums(u, v, h, rows, half_speed, edge, step):
    near, far = edge + step, edge + 2 * step
    sign = -1.0 if step > 0 else 1.0
    keep, cor, zonal = rows.keep(edge), rows.cor(edge), rows.zonal(edge)
    third, half = keep * (1.0 / 3.0), keep * 0.5
    hs, merid = sign * half_speed, sign * rows.merid(edge)
    vc_edge, vc_near, vc_far = (v[j] * rows.cos(j) for j in (edge, near, far))
    v1 = v[edge] - third * (cor * u[edge] + hs * h[near])
    h1 = h[edge] - third * (zonal * swap_parts(u[edge]) + merid * vc_near)
    u1 = u[edge] + third * (cor * v[edge] - zonal * swap_parts(h[edge]))
    near_third = rows.keep(near) * (1.0 / 3.0)
    near_v1 = v[near] - near_third * (rows.cor(near) * u[near] + hs * (h[far] - h[edge]))
    near_h1 = h[near] - near_third * (
        rows.zonal(near) * swap_parts(u[near]) + sign * rows.merid(near) * (vc_far - vc_edge)
    )
    v2 = v[edge] - half * (cor * u1 + hs * near_h1)
    h2 = h[edge] - half * (zonal * swap_parts(u1) + merid * (near_v1 * rows.cos(near)))
    return [v[edge], h[edge], v1, h1, v2, h2]


def field_dot(y_ref, x_ref, dft_ref, f, count):
    at = slice(f * count * 16, (f + 1) * count * 16)
    y_ref[at, :] = jnp.dot(x_ref[at, :], dft_ref[...], preferred_element_type=jnp.float32)


def forward_kernel(
    z_ref, dft_ref, tw_ref, cut_ref, speed_ref, slope_ref, least_ref, band_ref,
    own_ref, one_ref, two_ref, x_ref, y_ref,
):
    z = lax.axis_index("lat")
    even = lax.axis_index("lon_2") == 0
    sub, lane, inner = halves()
    inner4 = lax.broadcasted_iota(jnp.int32, (LV, 128), 1) % 64

    def slot(d, n):
        if n < SLOTS:
            return z_ref[d, n]
        return from_spare([z_ref[d, i] for i in range(3)], inner4)

    for f in range(3):
        spec = real_fft(
            [jnp.concatenate([slot(d, 2 * f), slot(d, 2 * f + 1)], axis=0) for d in range(NB)]
        )
        for k in range(NK):
            a, b = spec[k]
            c, s = tw_ref[k, 0:1, :], tw_ref[k, 1:2, :]
            if b is None:
                re, im = a * c, -(a * s)
            else:
                re, im = a * c + b * s, b * c - a * s
            split_store(x_ref, slice((f * NK + k) * 16, (f * NK + k) * 16 + 16), re, im)
        field_dot(y_ref, x_ref, dft_ref, f, NK)
    speed = speed_ref[...]
    turn_speed = jnp.where(sub, -speed, speed)
    half_speed = 0.5 * speed
    spare = {}
    for i in reversed(range(PAIRS)):
        tiles = []
        for f in range(3):
            parts = []
            for k in (2 * i, 2 * i + 1):
                if k == NK:
                    parts.append((jnp.zeros((8, 128), jnp.float32),) * 2)
                    continue
                at = (f * NK + k) * 16
                re = y_ref[at : at + 8, :128] + y_ref[at + 8 : at + 16, 128:]
                im = y_ref[at + 8 : at + 16, :128] - y_ref[at : at + 8, 128:]
                parts.append(swap_sub(re, im, sub))
            rows = []
            for half in range(2):
                rows += swap_lane(parts[0][half], parts[1][half], lane)
            for j in range(ROWS):
                own_ref[(i * 3 + f) * ROWS + j] = rows[j]
            tiles.append(rows)
        u, v, h = tiles
        rows = Rows(z, i, cut_ref, speed, turn_speed, slope_ref, least_ref, band_ref)
        to_south = edge_sums(u, v, h, rows, half_speed, ROWS - 1, -1)
        to_north = edge_sums(u, v, h, rows, half_speed, 0, 1)
        for n, (south, north) in enumerate(zip(to_south, to_north)):
            t = i * 6 + n
            for ref, tile in (
                (one_ref, jnp.where(even, south, north)),
                (two_ref, jnp.where(even, north, south)),
            ):
                if t >= SENT:
                    spare[ref is one_ref, t - SENT] = tile
                elif t < 3 * (PAIRS * 6 - SENT):
                    extra = spare_roll(spare[ref is one_ref, t // 3], t % 3)
                    ref[t] = jnp.where(inner < 48, tile, extra)
                else:
                    ref[t] = tile


def step_kernel(
    own_ref, one_ref, two_ref, cut_ref, speed_ref, slope_ref, least_ref, band_ref, dft_ref, tw_ref,
    w_ref, x_ref, y_ref, hold_ref,
):
    z = lax.axis_index("lat")
    even = lax.axis_index("lon_2") == 0
    sub, lane, inner = halves()
    speed = speed_ref[...]
    turn_speed = jnp.where(sub, -speed, speed)
    half_speed = 0.5 * speed

    def received(a_ref, b_ref, i):
        pick = lambda t: jnp.where(even, a_ref[t], b_ref[t])
        tiles = []
        for t in range(i * 6, i * 6 + 6):
            e = 3 * (t - SENT)
            tiles.append(pick(t) if t < SENT else from_spare([pick(e + c) for c in range(3)], inner))
        return tiles

    for i in range(PAIRS):
        above, below = received(one_ref, two_ref, i), received(two_ref, one_ref, i)
        u, v, h = ([own_ref[(i * 3 + f) * ROWS + j] for j in range(ROWS)] for f in range(3))
        rows = Rows(z, i, cut_ref, speed, turn_speed, slope_ref, least_ref, band_ref)
        span = range(-1, ROWS + 1)
        keep = {j: rows.keep(j) for j in span}
        zonal = {j: rows.zonal(j) for j in range(ROWS)}

        def advance(state, level, scale):
            su, sv, sh = state[:3]
            sv, sh = {j: sv[j] for j in range(ROWS)}, {j: sh[j] for j in range(ROWS)}
            before, after = above[2 * level : 2 * level + 2], below[2 * level : 2 * level + 2]
            if level == 0:
                (sv[-1], sh[-1]), (sv[ROWS], sh[ROWS]) = before, after
            else:
                last = ROWS - 1
                top, end = keep[-1] * state[3], keep[ROWS] * state[3]
                pv, ph = state[4]
                sv[-1] = before[0] + top * half_speed * ph[0]
                sh[-1] = before[1] + top * rows.merid(-1) * (pv[0] * rows.cos(0))
                sv[ROWS] = after[0] - end * half_speed * ph[last]
                sh[ROWS] = after[1] - end * rows.merid(ROWS) * (pv[last] * rows.cos(last))
            vc = {j: sv[j] * rows.cos(j) for j in span}
            out = [], [], []
            for j in range(ROWS):
                cor = rows.cor(j)
                tu = cor * sv[j] - zonal[j] * swap_parts(sh[j])
                tv = cor * su[j] + half_speed * (sh[j - 1] - sh[j + 1])
                th = zonal[j] * swap_parts(su[j]) + rows.merid(j) * (vc[j - 1] - vc[j + 1])
                if scale is None:
                    values = keep[j] * tu, -keep[j] * tv, -keep[j] * th
                else:
                    m = keep[j] * scale
                    values = u[j] + m * tu, v[j] - m * tv, h[j] - m * th
                for into, value in zip(out, values):
                    into.append(value)
            return *out, scale, (sv, sh)

        gain = advance((u, v, h), 0, 1.0 / 3.0)
        gain = advance(gain, 1, 0.5)
        gain = advance(gain, 2, None)
        for f in range(3):
            r = gain[f]
            north, south = swap_lane(r[0], r[1], lane), swap_lane(r[2], r[3], lane)
            for side in range(min(2, NK - 2 * i)):
                re, im = swap_sub(north[side], south[side], sub)
                at = (f * NK + 2 * i + side) * 16
                split_store(x_ref, pl.ds(at, 16), re, im)
    for f in (2, 0, 1):
        field_dot(y_ref, x_ref, dft_ref, f, NK)
        spec = []
        for k in range(NK):
            at = (f * NK + k) * 16
            a = y_ref[at : at + 8, :128] - y_ref[at + 8 : at + 16, 128:]
            b = y_ref[at + 8 : at + 16, :128] + y_ref[at : at + 8, 128:]
            c, s = tw_ref[k, 0:1, :], tw_ref[k, 1:2, :]
            spec.append((a * c - b * s, a * s + b * c))
        for d, value in enumerate(real_ifft(spec)):
            if f == 2:
                w_ref[d, 4] = value[:LV]
                low = pltpu.roll(value, LV, 0)
                hold_ref[d] = jnp.where(sub, low, value)
                continue
            extra = hold_ref[d]
            if f == 0:
                extra = jnp.where(sub, spare_roll(extra, 0), spare_roll(extra, 1))
                value = jnp.where(inner < 48, value, extra)
            else:
                extra = spare_roll(extra, 2)
                value = jnp.where(jnp.logical_and(sub, inner >= 48), extra, value)
            w_ref[d, 2 * f] = value[:LV]
            w_ref[d, 2 * f + 1] = value[LV:]


def unpack_kernel(w_ref, u_ref, v_ref, h_ref, u_hbm, v_hbm, h_hbm, out, sem):
    copies = []
    inner = lax.broadcasted_iota(jnp.int32, (128, 128), 1) % 64

    def slot(n):
        if n == SLOTS:
            return from_spare([slot(i) for i in range(3)], inner)
        return jnp.concatenate([w_ref[:, n, l, :] for l in range(LV)], axis=0)

    for f, (ref, hbm) in enumerate(((u_ref, u_hbm), (v_ref, v_hbm), (h_ref, h_hbm))):
        for half in range(2):
            turned = slot(2 * f + half).T
            for side in range(2):
                j = half * 2 + side
                out[f, :, j, :] = ref[:, j, :] + turned[side * 64 : side * 64 + NR, :]
        copies.append(pltpu.make_async_copy(out.at[f], hbm, sem.at[f]))
        copies[-1].start()
    for copy in copies:
        copy.wait()


def vmem(count):
    return [pl.BlockSpec(memory_space=pltpu.VMEM)] * count


def hbm(count):
    return [pl.BlockSpec(memory_space=pltpu.HBM)] * count


def shaped(*dims):
    return jax.ShapeDtypeStruct(dims, jnp.float32)


def shards(u_wind, v_wind, height, wave_speed, cutoff):
    bands = lax.axis_size("lat")
    dft, twid, twid_back, slope, least, per_band = host_tables(bands)
    levels = u_wind.shape[2]
    packed, cut_rows, speeds = pl.pallas_call(
        pack_kernel,
        out_shape=(
            shaped(NB, SLOTS, LV, 128),
            jax.ShapeDtypeStruct((16, 128), jnp.int32),
            shaped(8, 128),
        ),
        in_specs=hbm(5),
        out_specs=tuple(vmem(3)),
        scratch_shapes=[
            pltpu.VMEM((3, NR, ROWS, levels), jnp.float32),
            pltpu.VMEM((3, 2, 128, levels), jnp.float32),
            pltpu.SMEM(cutoff.shape, jnp.int32),
            pltpu.SMEM(wave_speed.shape, jnp.float32),
            pltpu.SemaphoreType.DMA((5,)),
        ],
        name="pack",
        compiler_params=PARAMS,
    )(*(pltpu.with_memory_space_constraint(a, pltpu.HBM) for a in (u_wind, v_wind, height, cutoff, wave_speed)))
    circles = lax.all_to_all(packed, LON, 0, 0, tiled=True)
    own, one, two = pl.pallas_call(
        forward_kernel,
        out_shape=(
            shaped(PAIRS * 3 * ROWS, 8, 128),
            shaped(SENT, 8, 128),
            shaped(SENT, 8, 128),
        ),
        in_specs=vmem(8),
        out_specs=tuple(vmem(3)),
        scratch_shapes=[
            pltpu.VMEM((3 * NK * 16, 768), jnp.bfloat16),
            pltpu.VMEM((3 * NK * 16, 256), jnp.float32),
        ],
        name="forward",
        compiler_params=PARAMS,
    )(circles, dft, twid, cut_rows, speeds, slope, least, per_band)
    stop = bands - 1
    south = [[(2 * i + c, 2 * i + 2 + c) for i in range(stop)] for c in range(2)]
    north = [[(b, a) for a, b in pairs] for pairs in south]
    one = lax.ppermute(one, ("lat", "lon_2"), south[0] + north[1])
    two = lax.ppermute(two, ("lat", "lon_2"), north[0] + south[1])
    waves = pl.pallas_call(
        step_kernel,
        out_shape=shaped(NB, SLOTS, LV, 128),
        in_specs=vmem(10),
        out_specs=vmem(1)[0],
        scratch_shapes=[
            pltpu.VMEM((3 * NK * 16, 768), jnp.bfloat16),
            pltpu.VMEM((3 * NK * 16, 256), jnp.float32),
            pltpu.VMEM((NB, 2 * LV, 128), jnp.float32),
        ],
        name="sections",
        compiler_params=PARAMS,
    )(own, one, two, cut_rows, speeds, slope, least, per_band, dft, twid_back)
    waves = lax.all_to_all(waves, LON, 0, 0, tiled=True)
    return pl.pallas_call(
        unpack_kernel,
        out_shape=tuple(shaped(NR, ROWS, levels) for _ in range(3)),
        in_specs=vmem(4),
        out_specs=tuple(hbm(3)),
        scratch_shapes=[
            pltpu.VMEM((3, NR, ROWS, levels), jnp.float32),
            pltpu.SemaphoreType.DMA((3,)),
        ],
        name="unpack",
        compiler_params=PARAMS,
    )(waves, u_wind, v_wind, height)


def solution(mesh):
    split = Mesh(
        mesh.devices.reshape(mesh.shape["lat"], 4, 4, 2), ("lat", "lon_0", "lon_1", "lon_2")
    )
    return jax.shard_map(
        shards,
        mesh=split,
        in_specs=(P(LON, "lat", None), P(LON, "lat", None), P(LON, "lat", None), P(), P()),
        out_specs=(P(LON, "lat", None), P(LON, "lat", None), P(LON, "lat", None)),
        check_vma=False,
    )
```

```python
import math

import jax
import jax.numpy as jnp
import ml_dtypes
import numpy as np
from jax import lax
from jax.experimental import pallas as pl
from jax.experimental.pallas import tpu as pltpu
from jax.sharding import Mesh
from jax.sharding import PartitionSpec as P

LON = ("lon_0", "lon_1", "lon_2")

NB = 32
NR = 45
PTS = NB * NR
NK = NB // 2 + 1
PAIRS = (NK + 1) // 2
ROWS = 4
HALO = 3
LV = 4
SLOTS = 5
SENT = 41
FAR = 1 << 20
PARAMS = pltpu.CompilerParams(vmem_limit_bytes=12 << 20)


def split_three(a):
    high = a.astype(ml_dtypes.bfloat16)
    rest = a - high.astype(np.float64)
    mid = rest.astype(ml_dtypes.bfloat16)
    low = (rest - mid.astype(np.float64)).astype(ml_dtypes.bfloat16)
    return high, mid, low


def host_tables(bands):
    r = np.arange(NR)
    ang = 2.0 * np.pi * np.outer(r, r) / NR
    dft = np.zeros((128, 256))
    twid = np.zeros((NK, 2, 128))
    for side in range(2):
        at = slice(side * 64, side * 64 + NR)
        dft[at, at] = np.cos(ang)
        dft[at, 128 + side * 64 : 128 + side * 64 + NR] = np.sin(ang)
        for k in range(NK):
            twid[k, 0, at] = np.cos(2.0 * np.pi * k * r / PTS)
            twid[k, 1, at] = np.sin(2.0 * np.pi * k * r / PTS)
    high, mid, low = split_three(dft)
    dft = np.concatenate([high, high, mid, mid, low, high], axis=0)
    lane = np.arange(128)
    k1 = 2 * np.arange(PAIRS)[:, None] + lane[None, :] // 64
    wav = k1 + NB * (lane % 64)[None, :]
    ok = (k1 < NK) & (lane % 64 < NR)[None, :]
    slope = np.where(ok, np.sin(2.0 * np.pi * wav / PTS), 0.0)
    least = np.where(ok, np.minimum(wav, PTS - wav), FAR)
    total = bands * ROWS
    per_band = np.zeros((bands, 4, 16, 128), np.float32)
    row = np.arange(-HALO, ROWS + HALO)
    half_pi = np.float32(0.5 * math.pi)
    for z in range(bands):
        g = z * ROWS + row
        ok = (g >= 0) & (g < total)
        lat = half_pi - (g.astype(np.float32) + np.float32(0.5)) * np.float32(math.pi / total)
        cos = np.where(ok, np.cos(lat, dtype=np.float32), np.float32(1.0))
        sin = np.sin(lat, dtype=np.float32)
        rows = (0.25 * sin, PTS / (2.0 * total) / cos, cos, 0.5 / cos)
        for c, value in enumerate(rows):
            per_band[z, c, : len(row), :] = np.where(ok, value, 0.0)[:, None]
    f32 = lambda a: jnp.asarray(np.asarray(a, np.float32))
    return (
        jnp.asarray(dft),
        f32(twid),
        f32(twid / PTS),
        f32(slope[:, None, :]),
        jnp.asarray(least[:, None, :].astype(np.int32)),
        f32(per_band),
    )


def real_fft(xs):
    n = len(xs)
    if n == 1:
        return [(xs[0], None)]
    even, odd = real_fft(xs[0::2]), real_fft(xs[1::2])
    out = [None] * (n // 2 + 1)
    for k in range(n // 4 + 1 if n > 2 else 1):
        er, ei = even[k]
        orr, oi = odd[k]
        if k == 0:
            out[0] = (er + orr, None)
            out[n // 2] = (er - orr, None)
        elif 4 * k == n:
            out[k] = (er, -orr)
        else:
            c, s = math.cos(2 * math.pi * k / n), math.sin(2 * math.pi * k / n)
            if oi is None:
                tr, ti = orr * c, orr * (-s)
            elif 8 * k == n:
                tr, ti = (orr + oi) * c, (oi - orr) * c
            else:
                tr, ti = orr * c + oi * s, oi * c - orr * s
            if ei is None:
                out[k] = (er + tr, ti)
                out[n // 2 - k] = (er - tr, ti)
            else:
                out[k] = (er + tr, ei + ti)
                out[n // 2 - k] = (er - tr, ti - ei)
    return out


def real_ifft(spec):
    n = 2 * (len(spec) - 1)
    if n == 2:
        return [spec[0][0] + spec[1][0], spec[0][0] - spec[1][0]]
    even, odd = [None] * (n // 4 + 1), [None] * (n // 4 + 1)
    for k in range(n // 4 + 1):
        ar, ai = spec[k]
        if k == 0:
            br = spec[n // 2][0]
            even[0] = (ar + br, None)
            odd[0] = (ar - br, None)
        elif 4 * k == n:
            even[k] = (2.0 * ar, None)
            odd[k] = (-2.0 * ai, None)
        else:
            br, bi = spec[n // 2 - k]
            even[k] = (ar + br, ai - bi)
            dr, di = ar - br, ai + bi
            c, s = math.cos(2 * math.pi * k / n), math.sin(2 * math.pi * k / n)
            if 8 * k == n:
                odd[k] = ((dr - di) * c, (dr + di) * c)
            else:
                odd[k] = (dr * c - di * s, dr * s + di * c)
    xe, xo = real_ifft(even), real_ifft(odd)
    out = []
    for a, b in zip(xe, xo):
        out += [a, b]
    return out


def pack_kernel(u_hbm, v_hbm, h_hbm, cut_hbm, speed_hbm, o_ref, cut_ref, speed_ref, raw, tmp, cut, speed, sem):
    fields = [
        pltpu.make_async_copy(src, raw.at[f], sem.at[f])
        for f, src in ((2, h_hbm), (0, u_hbm), (1, v_hbm))
    ]
    small = [
        pltpu.make_async_copy(cut_hbm, cut, sem.at[3]),
        pltpu.make_async_copy(speed_hbm, speed, sem.at[4]),
    ]
    for copy in fields + small:
        copy.start()
    for side in (0, 64):
        tmp[:, :, side + 40 : side + 64, :] = jnp.zeros((3, 2, 24, 128), jnp.float32)
    inner = lax.broadcasted_iota(jnp.int32, (128, 128), 1) % 64
    extra = None
    for f, copy in zip((2, 0, 1), fields):
        copy.wait()
        for j in range(ROWS):
            tmp[f, j // 2, j % 2 * 64 : j % 2 * 64 + NR, :] = raw[f, :, j, :]
        for half in (1, 0):
            n = 2 * f + half
            turned = tmp[f, half].T
            if n == SLOTS:
                extra = turned
                continue
            if n < 3:
                turned = jnp.where(inner < 48, turned, spare_roll(extra, n))
            for l in range(LV):
                o_ref[:, n, l, :] = turned[l * NB : (l + 1) * NB, :]
    for copy in small:
        copy.wait()
    z = lax.axis_index("lat")
    p = (lax.axis_index("lon_0") * 4 + lax.axis_index("lon_1")) * 2 + lax.axis_index("lon_2")
    total = cut.shape[0]
    sub = lax.broadcasted_iota(jnp.int32, (16, 128), 0)
    rows = jnp.full((16, 128), -1, jnp.int32)
    for i in range(ROWS + 2 * HALO):
        g = z * ROWS + i - HALO
        inside = jnp.logical_and(g >= 0, g < total)
        rows = jnp.where(sub == i, jnp.where(inside, cut[jnp.clip(g, 0, total - 1)], -1), rows)
    cut_ref[...] = rows
    sub = lax.broadcasted_iota(jnp.int32, (8, 128), 0)
    value = jnp.zeros((8, 128), jnp.float32)
    for l in range(LV):
        value = jnp.where(sub % LV == l, speed[l * NB + p], value)
    speed_ref[...] = value


def spare_roll(a, n):
    return pltpu.roll(a, 48 - 16 * n, 1)


def from_spare(tiles, inner):
    one, two, three = (pltpu.roll(t, 128 - 48 + 16 * n, 1) for n, t in enumerate(tiles))
    return jnp.where(inner < 16, one, jnp.where(inner < 32, two, three))


def split_store(ref, at, re, im):
    x = jnp.concatenate([re, im], axis=0)
    high = x.astype(jnp.bfloat16)
    rest = x - high.astype(jnp.float32)
    mid = rest.astype(jnp.bfloat16)
    low = (rest - mid.astype(jnp.float32)).astype(jnp.bfloat16)
    for i, part in enumerate((high, mid, high, mid, high, low)):
        ref[at, i * 128 : (i + 1) * 128] = part


def swap_sub(a, b, low):
    return jnp.where(low, a, pltpu.roll(b, 4, 0)), jnp.where(low, pltpu.roll(a, 4, 0), b)


def swap_lane(a, b, low):
    return jnp.where(low, a, pltpu.roll(b, 64, 1)), jnp.where(low, pltpu.roll(a, 64, 1), b)


def halves():
    sub = lax.broadcasted_iota(jnp.int32, (8, 128), 0) < 4
    lane = lax.broadcasted_iota(jnp.int32, (8, 128), 1)
    return sub, lane < 64, lane % 64


class Rows:
    def __init__(self, z, i, cut_ref, speed, turn_speed, slope_ref, least_ref, band_ref):
        self.z, self.cut, self.band, self.speed = z, cut_ref, band_ref, speed
        self.least, self.wave = least_ref[i], turn_speed * slope_ref[i]

    def of(self, c, row):
        return self.band[self.z, c, row + HALO : row + HALO + 1, :]

    def keep(self, row):
        kept = self.least <= self.cut[row + HALO : row + HALO + 1, :]
        return jnp.where(kept, 1.0, 0.0)

    def cor(self, row):
        return self.of(0, row)

    def zonal(self, row):
        return self.wave * self.of(1, row)

    def cos(self, row):
        return self.of(2, row)

    def merid(self, row):
        return self.speed * self.of(3, row)


def swap_parts(a):
    return pltpu.roll(a, LV, 0)


def edge_sums(u, v, h, rows, half_speed, edge, step):
    near, far = edge + step, edge + 2 * step
    sign = -1.0 if step > 0 else 1.0
    keep, cor, zonal = rows.keep(edge), rows.cor(edge), rows.zonal(edge)
    third, half = keep * (1.0 / 3.0), keep * 0.5
    hs, merid = sign * half_speed, sign * rows.merid(edge)
    vc_edge, vc_near, vc_far = (v[j] * rows.cos(j) for j in (edge, near, far))
    v1 = v[edge] - third * (cor * u[edge] + hs * h[near])
    h1 = h[edge] - third * (zonal * swap_parts(u[edge]) + merid * vc_near)
    u1 = u[edge] + third * (cor * v[edge] - zonal * swap_parts(h[edge]))
    near_third = rows.keep(near) * (1.0 / 3.0)
    near_v1 = v[near] - near_third * (rows.cor(near) * u[near] + hs * (h[far] - h[edge]))
    near_h1 = h[near] - near_third * (
        rows.zonal(near) * swap_parts(u[near]) + sign * rows.merid(near) * (vc_far - vc_edge)
    )
    v2 = v[edge] - half * (cor * u1 + hs * near_h1)
    h2 = h[edge] - half * (zonal * swap_parts(u1) + merid * (near_v1 * rows.cos(near)))
    return [v[edge], h[edge], v1, h1, v2, h2]


def field_dot(y_ref, x_ref, dft_ref, f, count):
    at = slice(f * count * 16, (f + 1) * count * 16)
    y_ref[at, :] = jnp.dot(x_ref[at, :], dft_ref[...], preferred_element_type=jnp.float32)


def forward_kernel(
    z_ref, dft_ref, tw_ref, cut_ref, speed_ref, slope_ref, least_ref, band_ref,
    own_ref, one_ref, two_ref, x_ref, y_ref,
):
    z = lax.axis_index("lat")
    even = lax.axis_index("lon_2") == 0
    sub, lane, inner = halves()
    inner4 = lax.broadcasted_iota(jnp.int32, (LV, 128), 1) % 64

    def slot(d, n):
        if n < SLOTS:
            return z_ref[d, n]
        return from_spare([z_ref[d, i] for i in range(3)], inner4)

    for f in range(3):
        spec = real_fft(
            [jnp.concatenate([slot(d, 2 * f), slot(d, 2 * f + 1)], axis=0) for d in range(NB)]
        )
        for k in range(NK):
            a, b = spec[k]
            c, s = tw_ref[k, 0:1, :], tw_ref[k, 1:2, :]
            if b is None:
                re, im = a * c, -(a * s)
            else:
                re, im = a * c + b * s, b * c - a * s
            split_store(x_ref, slice((f * NK + k) * 16, (f * NK + k) * 16 + 16), re, im)
        field_dot(y_ref, x_ref, dft_ref, f, NK)
    speed = speed_ref[...]
    turn_speed = jnp.where(sub, -speed, speed)
    half_speed = 0.5 * speed
    spare = {}
    for i in reversed(range(PAIRS)):
        tiles = []
        for f in range(3):
            parts = []
            for k in (2 * i, 2 * i + 1):
                if k == NK:
                    parts.append((jnp.zeros((8, 128), jnp.float32),) * 2)
                    continue
                at = (f * NK + k) * 16
                re = y_ref[at : at + 8, :128] + y_ref[at + 8 : at + 16, 128:]
                im = y_ref[at + 8 : at + 16, :128] - y_ref[at : at + 8, 128:]
                parts.append(swap_sub(re, im, sub))
            rows = []
            for half in range(2):
                rows += swap_lane(parts[0][half], parts[1][half], lane)
            for j in range(ROWS):
                own_ref[(i * 3 + f) * ROWS + j] = rows[j]
            tiles.append(rows)
        u, v, h = tiles
        rows = Rows(z, i, cut_ref, speed, turn_speed, slope_ref, least_ref, band_ref)
        to_south = edge_sums(u, v, h, rows, half_speed, ROWS - 1, -1)
        to_north = edge_sums(u, v, h, rows, half_speed, 0, 1)
        for n, (south, north) in enumerate(zip(to_south, to_north)):
            t = i * 6 + n
            for ref, tile in (
                (one_ref, jnp.where(even, south, north)),
                (two_ref, jnp.where(even, north, south)),
            ):
                if t >= SENT:
                    spare[ref is one_ref, t - SENT] = tile
                elif t < 3 * (PAIRS * 6 - SENT):
                    extra = spare_roll(spare[ref is one_ref, t // 3], t % 3)
                    ref[t] = jnp.where(inner < 48, tile, extra)
                else:
                    ref[t] = tile


def step_kernel(
    own_ref, one_ref, two_ref, cut_ref, speed_ref, slope_ref, least_ref, band_ref, dft_ref, tw_ref,
    w_ref, x_ref, y_ref, hold_ref,
):
    z = lax.axis_index("lat")
    even = lax.axis_index("lon_2") == 0
    sub, lane, inner = halves()
    speed = speed_ref[...]
    turn_speed = jnp.where(sub, -speed, speed)
    half_speed = 0.5 * speed

    def received(a_ref, b_ref, i):
        pick = lambda t: jnp.where(even, a_ref[t], b_ref[t])
        tiles = []
        for t in range(i * 6, i * 6 + 6):
            e = 3 * (t - SENT)
            tiles.append(pick(t) if t < SENT else from_spare([pick(e + c) for c in range(3)], inner))
        return tiles

    for i in range(PAIRS):
        above, below = received(one_ref, two_ref, i), received(two_ref, one_ref, i)
        u, v, h = ([own_ref[(i * 3 + f) * ROWS + j] for j in range(ROWS)] for f in range(3))
        rows = Rows(z, i, cut_ref, speed, turn_speed, slope_ref, least_ref, band_ref)
        span = range(-1, ROWS + 1)
        keep = {j: rows.keep(j) for j in span}
        zonal = {j: rows.zonal(j) for j in range(ROWS)}

        def advance(state, level, scale):
            su, sv, sh = state[:3]
            sv, sh = {j: sv[j] for j in range(ROWS)}, {j: sh[j] for j in range(ROWS)}
            before, after = above[2 * level : 2 * level + 2], below[2 * level : 2 * level + 2]
            if level == 0:
                (sv[-1], sh[-1]), (sv[ROWS], sh[ROWS]) = before, after
            else:
                last = ROWS - 1
                top, end = keep[-1] * state[3], keep[ROWS] * state[3]
                pv, ph = state[4]
                sv[-1] = before[0] + top * half_speed * ph[0]
                sh[-1] = before[1] + top * rows.merid(-1) * (pv[0] * rows.cos(0))
                sv[ROWS] = after[0] - end * half_speed * ph[last]
                sh[ROWS] = after[1] - end * rows.merid(ROWS) * (pv[last] * rows.cos(last))
            vc = {j: sv[j] * rows.cos(j) for j in span}
            out = [], [], []
            for j in range(ROWS):
                cor = rows.cor(j)
                tu = cor * sv[j] - zonal[j] * swap_parts(sh[j])
                tv = cor * su[j] + half_speed * (sh[j - 1] - sh[j + 1])
                th = zonal[j] * swap_parts(su[j]) + rows.merid(j) * (vc[j - 1] - vc[j + 1])
                if scale is None:
                    values = keep[j] * tu, -keep[j] * tv, -keep[j] * th
                else:
                    m = keep[j] * scale
                    values = u[j] + m * tu, v[j] - m * tv, h[j] - m * th
                for into, value in zip(out, values):
                    into.append(value)
            return *out, scale, (sv, sh)

        gain = advance((u, v, h), 0, 1.0 / 3.0)
        gain = advance(gain, 1, 0.5)
        gain = advance(gain, 2, None)
        for f in range(3):
            r = gain[f]
            north, south = swap_lane(r[0], r[1], lane), swap_lane(r[2], r[3], lane)
            for side in range(min(2, NK - 2 * i)):
                re, im = swap_sub(north[side], south[side], sub)
                at = (f * NK + 2 * i + side) * 16
                split_store(x_ref, pl.ds(at, 16), re, im)
    for f in (2, 0, 1):
        field_dot(y_ref, x_ref, dft_ref, f, NK)
        spec = []
        for k in range(NK):
            at = (f * NK + k) * 16
            a = y_ref[at : at + 8, :128] - y_ref[at + 8 : at + 16, 128:]
            b = y_ref[at + 8 : at + 16, :128] + y_ref[at : at + 8, 128:]
            c, s = tw_ref[k, 0:1, :], tw_ref[k, 1:2, :]
            spec.append((a * c - b * s, a * s + b * c))
        for d, value in enumerate(real_ifft(spec)):
            if f == 2:
                w_ref[d, 4] = value[:LV]
                low = pltpu.roll(value, LV, 0)
                hold_ref[d] = jnp.where(sub, low, value)
                continue
            extra = hold_ref[d]
            if f == 0:
                extra = jnp.where(sub, spare_roll(extra, 0), spare_roll(extra, 1))
                value = jnp.where(inner < 48, value, extra)
            else:
                extra = spare_roll(extra, 2)
                value = jnp.where(jnp.logical_and(sub, inner >= 48), extra, value)
            w_ref[d, 2 * f] = value[:LV]
            w_ref[d, 2 * f + 1] = value[LV:]


def unpack_kernel(w_ref, u_ref, v_ref, h_ref, u_hbm, v_hbm, h_hbm, out, sem):
    copies = []
    inner = lax.broadcasted_iota(jnp.int32, (128, 128), 1) % 64

    def slot(n):
        if n == SLOTS:
            return from_spare([slot(i) for i in range(3)], inner)
        return jnp.concatenate([w_ref[:, n, l, :] for l in range(LV)], axis=0)

    for f, (ref, hbm) in enumerate(((u_ref, u_hbm), (v_ref, v_hbm), (h_ref, h_hbm))):
        for half in range(2):
            turned = slot(2 * f + half).T
            for side in range(2):
                j = half * 2 + side
                out[f, :, j, :] = ref[:, j, :] + turned[side * 64 : side * 64 + NR, :]
        copies.append(pltpu.make_async_copy(out.at[f], hbm, sem.at[f]))
        copies[-1].start()
    for copy in copies:
        copy.wait()


def vmem(count):
    return [pl.BlockSpec(memory_space=pltpu.VMEM)] * count


def hbm(count):
    return [pl.BlockSpec(memory_space=pltpu.HBM)] * count


def shaped(*dims):
    return jax.ShapeDtypeStruct(dims, jnp.float32)


def shards(u_wind, v_wind, height, wave_speed, cutoff):
    bands = lax.axis_size("lat")
    dft, twid, twid_back, slope, least, per_band = host_tables(bands)
    levels = u_wind.shape[2]
    packed, cut_rows, speeds = pl.pallas_call(
        pack_kernel,
        out_shape=(
            shaped(NB, SLOTS, LV, 128),
            jax.ShapeDtypeStruct((16, 128), jnp.int32),
            shaped(8, 128),
        ),
        in_specs=hbm(5),
        out_specs=tuple(vmem(3)),
        scratch_shapes=[
            pltpu.VMEM((3, NR, ROWS, levels), jnp.float32),
            pltpu.VMEM((3, 2, 128, levels), jnp.float32),
            pltpu.SMEM(cutoff.shape, jnp.int32),
            pltpu.SMEM(wave_speed.shape, jnp.float32),
            pltpu.SemaphoreType.DMA((5,)),
        ],
        name="pack",
        compiler_params=PARAMS,
    )(*(pltpu.with_memory_space_constraint(a, pltpu.HBM) for a in (u_wind, v_wind, height, cutoff, wave_speed)))
    circles = lax.all_to_all(packed, LON, 0, 0, tiled=True)
    own, one, two = pl.pallas_call(
        forward_kernel,
        out_shape=(
            shaped(PAIRS * 3 * ROWS, 8, 128),
            shaped(SENT, 8, 128),
            shaped(SENT, 8, 128),
        ),
        in_specs=vmem(8),
        out_specs=tuple(vmem(3)),
        scratch_shapes=[
            pltpu.VMEM((3 * NK * 16, 768), jnp.bfloat16),
            pltpu.VMEM((3 * NK * 16, 256), jnp.float32),
        ],
        name="forward",
        compiler_params=PARAMS,
    )(circles, dft, twid, cut_rows, speeds, slope, least, per_band)
    stop = bands - 1
    south = [[(2 * i + c, 2 * i + 2 + c) for i in range(stop)] for c in range(2)]
    north = [[(b, a) for a, b in pairs] for pairs in south]
    one = lax.ppermute(one, ("lat", "lon_2"), south[0] + north[1])
    two = lax.ppermute(two, ("lat", "lon_2"), north[0] + south[1])
    waves = pl.pallas_call(
        step_kernel,
        out_shape=shaped(NB, SLOTS, LV, 128),
        in_specs=vmem(10),
        out_specs=vmem(1)[0],
        scratch_shapes=[
            pltpu.VMEM((3 * NK * 16, 768), jnp.bfloat16),
            pltpu.VMEM((3 * NK * 16, 256), jnp.float32),
            pltpu.VMEM((NB, 2 * LV, 128), jnp.float32),
        ],
        name="sections",
        compiler_params=PARAMS,
    )(own, one, two, cut_rows, speeds, slope, least, per_band, dft, twid_back)
    waves = lax.all_to_all(waves, LON, 0, 0, tiled=True)
    return pl.pallas_call(
        unpack_kernel,
        out_shape=tuple(shaped(NR, ROWS, levels) for _ in range(3)),
        in_specs=vmem(4),
        out_specs=tuple(hbm(3)),
        scratch_shapes=[
            pltpu.VMEM((3, NR, ROWS, levels), jnp.float32),
            pltpu.SemaphoreType.DMA((3,)),
        ],
        name="unpack",
        compiler_params=PARAMS,
    )(waves, u_wind, v_wind, height)


def solution(mesh):
    split = Mesh(
        mesh.devices.reshape(mesh.shape["lat"], 4, 4, 2), ("lat", "lon_0", "lon_1", "lon_2")
    )
    return jax.shard_map(
        shards,
        mesh=split,
        in_specs=(P(LON, "lat", None), P(LON, "lat", None), P(LON, "lat", None), P(), P()),
        out_specs=(P(LON, "lat", None), P(LON, "lat", None), P(LON, "lat", None)),
        check_vma=False,
    )
```
